512 devices in a mesh: dp: 16 (over z), expert: 32 (over x, y, core).
Axes of the slice: x: 4, y: 4, z: 16, core: 2. Of those that a mesh axis runs over, the one named last changes fastest.
Arguments:
- first_out: bfloat16 [65536, 1024], P(('dp', 'expert')), may hold values from -6 to 6
- second_out: bfloat16 [65536, 1024], P(('dp', 'expert')), may hold values from -6 to 6
- first_grad: bfloat16 [65536, 1024], P(('dp', 'expert')), may hold values from -6 to 6
- second_grad: bfloat16 [65536, 1024], P(('dp', 'expert')), may hold values from -6 to 6
- routes: int32 [65536, 2], P(('dp', 'expert')), may hold values from 0 to 31, all different within a row; in each aligned block of 128 rows (0 to 127, 128 to 255, ...) at most 16 rows name the same one
- gate_values: float32 [65536, 2], P(('dp', 'expert')), may hold values from 0.1 to 1
- w_gate: bfloat16 [32, 1024, 768], P('expert', 'dp'), may hold values from -0.1875 to 0.1875
- w_up: bfloat16 [32, 1024, 768], P('expert', 'dp'), may hold values from -0.1875 to 0.1875
- w_down: bfloat16 [32, 1024, 768], P('expert', 'dp'), may hold values from -0.21875 to 0.21875
Outputs:
- second_in: bfloat16 [65536, 1024], P(('dp', 'expert'))
- first_total: bfloat16 [65536, 1024], P(('dp', 'expert'))
- gate_grad: float32 [65536, 2], P(('dp', 'expert'))
- w_down_grad: float32 [32, 1024, 768], P('expert', 'dp')
The draws below stay inside these ranges and needn't reach their ends.
Inputs may be any that keep to these rules, and one draw needn't show every extreme that they name: `routes`: each row names 2 different experts. Among the 128 rows of one device no expert is named more than 16 times, and in every draw some device names some expert exactly 16 times.
All inputs are finite; a program needn't handle non-finite values.
Results may differ from the reference program's by a relative error of at most 0.0051.
Values may be sent and summed in bfloat16 or wider, within the bound.
No kernel may reach another device: no remote copies, remote signals or barrier semaphores. Data moves between devices by JAX's collectives and lax.ppermute only.
A program may use at most 64 MiB of HBM per device.

```python
import math
import jax
import jax.numpy as jnp
import numpy as np
from jax import lax

D = 1024
H = 768
TOP = 2
TOK_DEV = 128
EXPERTS = 32
CAP = 16
ROWS_COL = 2048
TOKENS = 65536


def level_of(rng, extent, pieces, smallest, largest):
    gain = 1.0
    for axis_at, blocks in pieces:
        draws = jax.random.uniform(jax.random.fold_in(jax.random.fold_in(rng, 6), axis_at), (blocks,), jnp.float32, smallest / len(pieces), largest / len(pieces))
        gain = gain * jnp.repeat(jnp.exp(draws), extent[axis_at] // blocks).reshape((-1,) + (1,) * (len(extent) - 1 - axis_at))
    return gain


def deal_out(rng, own, number, rows, count, top, reach, lean):
    sequence = jax.random.permutation(rng, count)
    heavy_load, usual = portions_of(count, rows * top, reach, lean, True), portions_of(count, rows * top, reach, lean, False)
    places = jnp.arange(count)

    def named(lengths, rotation):
        used = int((lengths > 0).sum())
        fixed = max(1, used // 4)
        moved = fixed + (places - fixed + rotation * (used - fixed)) % max(1, count - fixed)
        return jnp.zeros((count,), jnp.int32).at[sequence[jnp.where(places < fixed, places, moved)]].set(jnp.asarray(lengths, jnp.int32))

    lengths = jnp.where(number % 4 == 0, named(heavy_load, number // 4), named(usual, number - number // 4 - 1))
    mixed = jax.random.permutation(jax.random.fold_in(own, 3), count)
    donor, receiver = mixed[0:count // 2 * 2:2], mixed[1:count // 2 * 2:2]
    room = jnp.minimum(lengths[donor] - 1, reach - lengths[receiver]) // 2
    room = jnp.where((donor == sequence[0]) | (receiver == sequence[0]) | (lengths[receiver] == 0), 0, jnp.maximum(room, 0))
    moved = jax.random.randint(jax.random.fold_in(own, 4), (count // 2,), 0, 1 << 20) % (room + 1)
    lengths = lengths.at[donor].add(-moved).at[receiver].add(moved)
    members = jnp.searchsorted(jnp.cumsum(lengths), jnp.arange(rows * top), side="right").astype(jnp.int32)
    table = members.reshape(top, rows).T
    table = table[jax.random.permutation(jax.random.fold_in(own, 1), rows)]
    rotation = jax.random.randint(jax.random.fold_in(own, 2), (rows, 1), 0, top)
    return jnp.take_along_axis(table, (jnp.arange(top)[None, :] + rotation) % top, axis=1)


def portions_of(number_of, total, reach, slope, full):
    portions = [(1 << 20) // math.isqrt(grade ** slope) + 1 for grade in range(1, number_of + 1)]
    largest = reach if full else min(reach, max(-(-total // number_of), total * portions[0] // sum(portions)))
    least = 1 if total - largest >= number_of - 1 else 0
    given, spare = [largest] + [least] * (number_of - 1), total - largest - least * (number_of - 1)
    while spare > 0:
        movable = [i for i in range(1, number_of) if given[i] < largest] or [i for i in range(1, number_of) if given[i] < reach]
        mass, budget = sum([portions[i] for i in movable]), spare
        for i in movable:
            addition = min(reach - given[i], max(1, budget * portions[i] // mass), spare)
            given[i] = given[i] + addition
            spare = spare - addition
    return np.array(given)


def bell_draw(stream_key, shape, spread, bound, cuts=(), kind=jnp.bfloat16):
    level = level_of(stream_key, shape, cuts, -0.22, 0.18) if cuts else 1.0
    values = jax.random.normal(stream_key, shape, jnp.float32) * spread * level
    return jnp.minimum(jnp.maximum(values, -bound), bound).astype(kind)


def setup_inputs(seed: int = 0) -> dict:
    splits = jax.random.split(jax.random.key(seed), 10)
    first_out = bell_draw(splits[0], (TOKENS, D), 1.0, 6.0, ((0, 512),))
    second_out = bell_draw(splits[1], (TOKENS, D), 1.0, 6.0, ((0, 512),))
    first_grad = bell_draw(splits[2], (TOKENS, D), 1.0, 6.0, ((0, 512),))
    second_grad = bell_draw(splits[3], (TOKENS, D), 1.0, 6.0, ((0, 512),))
    routes_keys = jax.random.split(jax.random.fold_in(splits[4], 1), TOKENS // TOK_DEV)
    routes_turns = jax.random.permutation(jax.random.fold_in(splits[4], 3), TOKENS // TOK_DEV)
    routes = jax.vmap(lambda own, number: deal_out(jax.random.fold_in(splits[4], 2), own, number, TOK_DEV, EXPERTS, TOP, CAP, 2))(routes_keys, routes_turns).reshape((TOKENS, TOP))
    gate_values = jnp.clip(0.1 + 0.9 * jax.random.uniform(splits[5], (TOKENS, TOP), jnp.float32) ** level_of(splits[5], (TOKENS, TOP), ((0, 512),), -0.2, 0.2), 0.1, 1.0)
    w_gate = bell_draw(splits[6], (EXPERTS, D, H), D ** -0.5, 0.1875, ((0, 32), (1, 16)))
    w_up = bell_draw(splits[7], (EXPERTS, D, H), D ** -0.5, 0.1875, ((0, 32), (1, 16)))
    w_down = bell_draw(splits[8], (EXPERTS, D, H), H ** -0.5, 0.21875, ((0, 32), (1, 16)))
    return dict(first_out=first_out, second_out=second_out, first_grad=first_grad, second_grad=second_grad, routes=routes, gate_values=gate_values, w_gate=w_gate, w_up=w_up, w_down=w_down)


def expert_rows(rows_in, rows_cot, gate_mat, up_mat, down_mat):
    pre_gate = jnp.dot(rows_in, gate_mat, preferred_element_type=jnp.float32)
    pre_up = jnp.dot(rows_in, up_mat, preferred_element_type=jnp.float32)
    squashed = jax.nn.sigmoid(pre_gate)
    activated = pre_gate * squashed
    hidden = (activated * pre_up).astype(jnp.bfloat16)
    out_rows = lax.dot_general(hidden, down_mat, (((1,), (1,)), ((), ())), preferred_element_type=jnp.float32).astype(jnp.bfloat16)
    hidden_cot = jnp.dot(rows_cot, down_mat, preferred_element_type=jnp.float32)
    gate_cot = (hidden_cot * pre_up * squashed * (1.0 + pre_gate * (1.0 - squashed))).astype(jnp.bfloat16)
    up_cot = (hidden_cot * activated).astype(jnp.bfloat16)
    input_cot = lax.dot_general(gate_cot, gate_mat, (((1,), (1,)), ((), ())), preferred_element_type=jnp.float32)
    input_cot = input_cot + lax.dot_general(up_cot, up_mat, (((1,), (1,)), ((), ())), preferred_element_type=jnp.float32)
    return (out_rows, input_cot.astype(jnp.bfloat16), hidden)

def reference(first_out, second_out, first_grad, second_grad, routes, gate_values, w_gate, w_up, w_down):
    assigned = TOKENS * TOP
    expert_ids = routes.reshape(assigned).astype(jnp.int32)
    token_of = jnp.arange(assigned, dtype=jnp.int32) // TOP
    out_cot_all = (gate_values.reshape(assigned)[:, None] * second_grad[token_of].astype(jnp.float32)).astype(jnp.bfloat16)
    sort_order = jnp.argsort(expert_ids, stable=True).astype(jnp.int32)
    counts = lax.optimization_barrier(jnp.sum((expert_ids[:, None] == jnp.arange(EXPERTS, dtype=jnp.int32)[None, :]).astype(jnp.int32), axis=0))
    starts = (jnp.cumsum(counts) - counts).astype(jnp.int32)
    block_rows = 1024
    order_pad = jnp.concatenate([sort_order, jnp.full((block_rows,), assigned, jnp.int32)])

    def per_expert(scan_carry, inputs):
        first_start, row_count, gate_mat, up_mat, down_mat = inputs

        def per_block(block_step, loop_state):
            out_acc, cot_acc, grad_acc = loop_state
            offset = (block_step * block_rows).astype(jnp.int32)
            row_index = lax.dynamic_slice_in_dim(order_pad, (first_start + offset).astype(jnp.int32), block_rows)
            in_range = offset + jnp.arange(block_rows, dtype=jnp.int32) < row_count
            row_index = jnp.where(in_range, row_index, assigned).astype(jnp.int32)
            safe_index = jnp.minimum(row_index, assigned - 1)
            rows_in = jnp.where(in_range[:, None], first_out[safe_index // TOP], jnp.zeros((), jnp.bfloat16))
            rows_cot = jnp.where(in_range[:, None], out_cot_all[safe_index], jnp.zeros((), jnp.bfloat16))
            out_rows, input_cot, hidden = expert_rows(rows_in, rows_cot, gate_mat, up_mat, down_mat)
            grad_acc = grad_acc + lax.dot_general(rows_cot, hidden, (((0,), (0,)), ((), ())), preferred_element_type=jnp.float32)
            out_acc = out_acc.at[row_index].set(out_rows, mode='drop')
            cot_acc = cot_acc.at[row_index].set(input_cot, mode='drop')
            return (out_acc, cot_acc, grad_acc)
        blocks = (row_count + block_rows - 1) // block_rows
        out_acc, cot_acc, grad_acc = lax.fori_loop(0, blocks, per_block, (scan_carry[0], scan_carry[1], jnp.zeros((D, H), jnp.float32)))
        return ((out_acc, cot_acc), grad_acc)
    empty_rows = jnp.zeros((assigned, D), jnp.bfloat16)
    (out_acc, cot_acc), grad_stack = lax.scan(per_expert, (empty_rows, empty_rows), (starts, counts, w_gate, w_up, w_down))
    expert_out = out_acc.reshape(TOKENS, TOP, D).astype(jnp.float32)
    combined = lax.optimization_barrier(jnp.sum(gate_values[:, :, None] * expert_out, axis=1))
    second_in = (second_out.astype(jnp.float32) - combined).astype(jnp.bfloat16)
    gate_grad = lax.optimization_barrier(jnp.sum(second_grad.astype(jnp.float32)[:, None, :] * expert_out, axis=2))
    first_total = (first_grad.astype(jnp.float32) + lax.optimization_barrier(jnp.sum(cot_acc.reshape(TOKENS, TOP, D).astype(jnp.float32), axis=1))).astype(jnp.bfloat16)
    w_down_grad = grad_stack * (1.0 / math.sqrt(ROWS_COL))
    return (second_in, first_total, gate_grad, w_down_grad)
```

```python
import math

import jax
import jax.numpy as jnp
from jax import lax
from jax.sharding import PartitionSpec as P


def expert_rows(rows_in, rows_cot, gate_mat, up_mat, down_mat):
    pre_gate = jnp.dot(rows_in, gate_mat, preferred_element_type=jnp.float32)
    pre_up = jnp.dot(rows_in, up_mat, preferred_element_type=jnp.float32)
    squashed = jax.nn.sigmoid(pre_gate)
    activated = pre_gate * squashed
    hidden = (activated * pre_up).astype(jnp.bfloat16)
    out_rows = lax.dot_general(
        hidden, down_mat, (((1,), (1,)), ((), ())), preferred_element_type=jnp.float32
    ).astype(jnp.bfloat16)
    hidden_cot = jnp.dot(rows_cot, down_mat, preferred_element_type=jnp.float32)
    gate_cot = (hidden_cot * pre_up * squashed * (1.0 + pre_gate * (1.0 - squashed))).astype(
        jnp.bfloat16
    )
    up_cot = (hidden_cot * activated).astype(jnp.bfloat16)
    input_cot = lax.dot_general(
        gate_cot, gate_mat, (((1,), (1,)), ((), ())), preferred_element_type=jnp.float32
    )
    input_cot = input_cot + lax.dot_general(
        up_cot, up_mat, (((1,), (1,)), ((), ())), preferred_element_type=jnp.float32
    )
    return (out_rows, input_cot.astype(jnp.bfloat16), hidden)


def to_slots(placing, assigned_rows):
    return lax.dot_general(
        placing, assigned_rows, (((0,), (0,)), ((), ())), preferred_element_type=jnp.float32
    ).astype(jnp.bfloat16)


def per_device(
    first_out, second_out, first_grad, second_grad, routes, gate_values, w_gate, w_up, w_down
):
    count_here = first_out.shape[0]
    feature_count = first_out.shape[1]
    top_count = routes.shape[1]
    owners = lax.axis_size("expert")
    groups = lax.axis_size("dp")
    capacity = min(count_here, 2 * count_here * top_count // owners)
    assigned = count_here * top_count
    slots_all = owners * capacity
    expert_ids = routes.reshape(assigned)
    onehot = (expert_ids[:, None] == jnp.arange(owners, dtype=jnp.int32)[None, :]).astype(jnp.int32)
    before = jnp.cumsum(onehot, axis=0) - onehot
    rank_in = jnp.sum(before * onehot, axis=1)
    slot_index = expert_ids * capacity + rank_in
    placing = (slot_index[:, None] == jnp.arange(slots_all, dtype=jnp.int32)[None, :]).astype(
        jnp.bfloat16
    )
    repeated = jnp.broadcast_to(
        first_out[:, None, :], (count_here, top_count, feature_count)
    ).reshape(assigned, feature_count)
    grad_repeated = jnp.broadcast_to(
        second_grad[:, None, :], (count_here, top_count, feature_count)
    ).reshape(assigned, feature_count)
    cot_rows = (gate_values.reshape(assigned)[:, None] * grad_repeated.astype(jnp.float32)).astype(
        jnp.bfloat16
    )
    send_input = to_slots(placing, repeated).reshape(owners, capacity, feature_count)
    send_cot = to_slots(placing, cot_rows).reshape(owners, capacity, feature_count)
    arrived_input, arrived_cot = (
        lax.all_to_all(send_input, "expert", split_axis=0, concat_axis=0, tiled=True),
        lax.all_to_all(send_cot, "expert", split_axis=0, concat_axis=0, tiled=True),
    )
    rows_in = arrived_input.reshape(slots_all, feature_count)
    rows_cot = arrived_cot.reshape(slots_all, feature_count)
    hidden_count = w_gate.shape[2]
    shards = jnp.concatenate([w_gate[0], w_up[0], w_down[0]], axis=1)
    mats = lax.all_gather(shards, "dp", axis=0, tiled=True)
    gate_mat = mats[:, :hidden_count]
    up_mat = mats[:, hidden_count : 2 * hidden_count]
    down_mat = mats[:, 2 * hidden_count :]
    out_rows, input_cot, hidden = expert_rows(rows_in, rows_cot, gate_mat, up_mat, down_mat)
    grad_scale = 1.0 / math.sqrt(count_here * groups)
    partial_grad = lax.dot_general(
        rows_cot, hidden, (((0,), (0,)), ((), ())), preferred_element_type=jnp.float32
    )
    reduced = lax.psum_scatter(partial_grad, "dp", scatter_dimension=0, tiled=True)
    w_down_grad = (reduced * grad_scale)[None]
    back_out, back_cot = (
        lax.all_to_all(
            out_rows.reshape(owners, capacity, feature_count),
            "expert",
            split_axis=0,
            concat_axis=0,
            tiled=True,
        ),
        lax.all_to_all(
            input_cot.reshape(owners, capacity, feature_count),
            "expert",
            split_axis=0,
            concat_axis=0,
            tiled=True,
        ),
    )
    out_assigned = jnp.dot(
        placing, back_out.reshape(slots_all, feature_count), preferred_element_type=jnp.float32
    )
    cot_assigned = jnp.dot(
        placing, back_cot.reshape(slots_all, feature_count), preferred_element_type=jnp.float32
    )
    expert_out = out_assigned.reshape(count_here, top_count, feature_count)
    combined = jnp.sum(gate_values[:, :, None] * expert_out, axis=1)
    second_in = (second_out.astype(jnp.float32) - combined).astype(jnp.bfloat16)
    gate_grad = jnp.sum(second_grad.astype(jnp.float32)[:, None, :] * expert_out, axis=2)
    first_total = (
        first_grad.astype(jnp.float32)
        + jnp.sum(cot_assigned.reshape(count_here, top_count, feature_count), axis=1)
    ).astype(jnp.bfloat16)
    return (second_in, first_total, gate_grad, w_down_grad)


def solution(mesh):
    placed = (
        P(("dp", "expert"), None),
        P(("dp", "expert"), None),
        P(("dp", "expert"), None),
        P(("dp", "expert"), None),
        P(("dp", "expert"), None),
        P(("dp", "expert"), None),
        P("expert", "dp", None),
        P("expert", "dp", None),
        P("expert", "dp", None),
    )
    return jax.shard_map(
        per_device,
        mesh=mesh,
        in_specs=placed,
        out_specs=(
            P(("dp", "expert"), None),
            P(("dp", "expert"), None),
            P(("dp", "expert"), None),
            P("expert", "dp", None),
        ),
        check_vma=False,
    )
```

```python
import math

import jax
import jax.numpy as jnp
from jax import lax
from jax.experimental import pallas as pl
from jax.experimental.pallas import tpu as pltpu
from jax.sharding import PartitionSpec as P


BLOCK = 256
STRIDE = 4


def _dot(a, b, over):
    return lax.dot_general(a, b, ((over[:1], over[1:]), ((), ())), preferred_element_type=jnp.float32)


def _hidden_kernel(
    place, rows, cot, gate, up, hidden, slope, activated, send_two, send_one, own_three, own_zero, classes
):
    pre_gate = _dot(rows[...], gate[...], (1, 0))
    pre_up = _dot(rows[...], up[...], (1, 0))
    squashed = jax.nn.sigmoid(pre_gate)
    active = pre_gate * squashed
    here = (active * pre_up).astype(jnp.bfloat16)
    hidden[...] = here
    activated[...] = active
    slope[...] = pre_up * squashed * (1.0 + pre_gate * (1.0 - squashed))
    partial = _dot(cot[...], here, (0, 0))
    members, block = classes.shape[1], classes.shape[2]
    for index in range(members * STRIDE):
        classes[index % STRIDE, index // STRIDE] = partial[index * block : (index + 1) * block]
    for shift, target in ((2, send_two), (1, send_one), (3, own_three), (0, own_zero)):
        target[...] = classes[(place[0] + shift) % STRIDE].astype(target.dtype)


def hidden_and_partial(place, rows, cot, mats, groups):
    slots, features = rows.shape
    width = mats.shape[1] // 3
    steps = width // BLOCK
    members, block = groups // STRIDE, features // groups
    whole = pl.BlockSpec((slots, features), lambda j, place: (0, 0))
    column = pl.BlockSpec((slots, BLOCK), lambda j, place: (0, j))
    part = pl.BlockSpec((members, block, BLOCK), lambda j, place: (0, 0, j))
    part_shape = (members, block, width)
    return pl.pallas_call(
        _hidden_kernel,
        grid_spec=pltpu.PrefetchScalarGridSpec(
            num_scalar_prefetch=1,
            grid=(steps,),
            in_specs=[
                whole,
                whole,
                pl.BlockSpec((features, BLOCK), lambda j, place: (0, j)),
                pl.BlockSpec((features, BLOCK), lambda j, place: (0, j + steps)),
            ],
            out_specs=[column, column, column, part, part, part, part],
            scratch_shapes=[pltpu.VMEM((STRIDE, members, block, BLOCK), jnp.float32)],
        ),
        out_shape=[
            jax.ShapeDtypeStruct((slots, width), jnp.bfloat16),
            jax.ShapeDtypeStruct((slots, width), jnp.float32),
            jax.ShapeDtypeStruct((slots, width), jnp.float32),
            jax.ShapeDtypeStruct(part_shape, jnp.bfloat16),
            jax.ShapeDtypeStruct(part_shape, jnp.bfloat16),
            jax.ShapeDtypeStruct(part_shape, jnp.float32),
            jax.ShapeDtypeStruct(part_shape, jnp.float32),
        ],
        name="hidden_and_partial",
    )(place, rows, cot, mats, mats)


def _back_kernel(hidden, cot, slope, activated, gate, up, down_mat, back, out_sum, cot_sum):
    at = pl.program_id(0)
    features = cot.shape[1]
    down = down_mat[...]
    hidden_cot = _dot(cot[...], down, (1, 0))
    gate_cot = (hidden_cot * slope[...]).astype(jnp.bfloat16)
    up_cot = (hidden_cot * activated[...]).astype(jnp.bfloat16)
    out_part = _dot(hidden[...], down, (1, 1))
    cot_part = _dot(gate_cot, gate[...], (1, 1)) + _dot(up_cot, up[...], (1, 1))

    @pl.when(at == 0)
    def _():
        out_sum[...] = out_part
        cot_sum[...] = cot_part

    @pl.when(at > 0)
    def _():
        out_sum[...] += out_part
        cot_sum[...] += cot_part

    @pl.when(at == pl.num_programs(0) - 1)
    def _():
        back[:, :features] = out_sum[...].astype(jnp.bfloat16)
        back[:, features:] = cot_sum[...].astype(jnp.bfloat16)


def rows_back(hidden, cot, slope, activated, mats):
    slots, features = cot.shape
    steps = hidden.shape[1] // BLOCK
    column = pl.BlockSpec((slots, BLOCK), lambda j: (0, j))
    return pl.pallas_call(
        _back_kernel,
        grid=(steps,),
        in_specs=[
            column,
            pl.BlockSpec((slots, features), lambda j: (0, 0)),
            column,
            column,
            pl.BlockSpec((features, BLOCK), lambda j: (0, j)),
            pl.BlockSpec((features, BLOCK), lambda j: (0, j + steps)),
            pl.BlockSpec((features, BLOCK), lambda j: (0, j + 2 * steps)),
        ],
        out_specs=pl.BlockSpec((slots, 2 * features), lambda j: (0, 0)),
        out_shape=jax.ShapeDtypeStruct((slots, 2 * features), jnp.bfloat16),
        scratch_shapes=[
            pltpu.VMEM((slots, features), jnp.float32),
            pltpu.VMEM((slots, features), jnp.float32),
        ],
        name="rows_back",
    )(hidden, cot, slope, activated, mats, mats, mats)


def to_slots(placing, assigned_rows):
    return lax.dot_general(
        placing, assigned_rows, (((0,), (0,)), ((), ())), preferred_element_type=jnp.float32
    ).astype(jnp.bfloat16)


def window_reduce(send_two, send_one, own_three, own_zero, groups):
    members = groups // STRIDE
    place = lax.axis_index("dp")

    def moved(value, by):
        return lax.ppermute(value, "dp", [(i, (i + by) % groups) for i in range(groups)])

    from_second = moved(send_two, -1)
    from_below = moved(send_one, 1)
    passed_on = (from_second.astype(jnp.float32) + own_three).astype(jnp.bfloat16)
    from_above = moved(passed_on, -1)
    window = from_above.astype(jnp.float32) + (from_below.astype(jnp.float32) + own_zero)
    rounded = window.astype(jnp.bfloat16)
    member = place // STRIDE

    def block_of(values, ahead):
        return lax.dynamic_index_in_dim(values, (member + ahead) % members, 0, keepdims=False)

    total = block_of(window, 0)
    for ahead in range(1, members):
        total = total + moved(block_of(rounded, ahead), ahead * STRIDE).astype(jnp.float32)
    return total


def per_device(
    first_out, second_out, first_grad, second_grad, routes, gate_values, w_gate, w_up, w_down
):
    count_here = first_out.shape[0]
    feature_count = first_out.shape[1]
    top_count = routes.shape[1]
    owners = lax.axis_size("expert")
    groups = lax.axis_size("dp")
    capacity = min(count_here, 2 * count_here * top_count // owners)
    assigned = count_here * top_count
    slots_all = owners * capacity
    expert_ids = routes.reshape(assigned)
    onehot = (expert_ids[:, None] == jnp.arange(owners, dtype=jnp.int32)[None, :]).astype(jnp.int32)
    before = jnp.cumsum(onehot, axis=0) - onehot
    rank_in = jnp.sum(before * onehot, axis=1)
    slot_index = expert_ids * capacity + rank_in
    placing = (slot_index[:, None] == jnp.arange(slots_all, dtype=jnp.int32)[None, :]).astype(
        jnp.bfloat16
    )
    repeated = jnp.broadcast_to(
        first_out[:, None, :], (count_here, top_count, feature_count)
    ).reshape(assigned, feature_count)
    grad_repeated = jnp.broadcast_to(
        second_grad[:, None, :], (count_here, top_count, feature_count)
    ).reshape(assigned, feature_count)
    cot_rows = (gate_values.reshape(assigned)[:, None] * grad_repeated.astype(jnp.float32)).astype(
        jnp.bfloat16
    )
    send_input = to_slots(placing, repeated).reshape(owners, capacity, feature_count)
    send_cot = to_slots(placing, cot_rows).reshape(owners, capacity, feature_count)
    arrived_input, arrived_cot = (
        lax.all_to_all(send_input, "expert", split_axis=0, concat_axis=0, tiled=True),
        lax.all_to_all(send_cot, "expert", split_axis=0, concat_axis=0, tiled=True),
    )
    rows_in = arrived_input.reshape(slots_all, feature_count)
    rows_cot = arrived_cot.reshape(slots_all, feature_count)
    shards = jnp.concatenate([w_gate[0], w_up[0], w_down[0]], axis=1)
    mats = lax.all_gather(shards, "dp", axis=0, tiled=True)
    place = lax.axis_index("dp").astype(jnp.int32).reshape(1)
    hidden, slope, activated, *parts = hidden_and_partial(place, rows_in, rows_cot, mats, groups)
    back_rows = rows_back(hidden, rows_cot, slope, activated, mats)
    back = lax.all_to_all(
        back_rows.reshape(owners, capacity, 2 * feature_count),
        "expert",
        split_axis=0,
        concat_axis=0,
        tiled=True,
    ).reshape(slots_all, 2 * feature_count)
    grad_scale = 1.0 / math.sqrt(count_here * groups)
    w_down_grad = (window_reduce(*parts, groups) * grad_scale)[None]
    out_assigned = jnp.dot(placing, back[:, :feature_count], preferred_element_type=jnp.float32)
    cot_assigned = jnp.dot(placing, back[:, feature_count:], preferred_element_type=jnp.float32)
    expert_out = out_assigned.reshape(count_here, top_count, feature_count)
    combined = jnp.sum(gate_values[:, :, None] * expert_out, axis=1)
    second_in = (second_out.astype(jnp.float32) - combined).astype(jnp.bfloat16)
    gate_grad = jnp.sum(second_grad.astype(jnp.float32)[:, None, :] * expert_out, axis=2)
    first_total = (
        first_grad.astype(jnp.float32)
        + jnp.sum(cot_assigned.reshape(count_here, top_count, feature_count), axis=1)
    ).astype(jnp.bfloat16)
    return (second_in, first_total, gate_grad, w_down_grad)


def solution(mesh):
    placed = (
        P(("dp", "expert"), None),
        P(("dp", "expert"), None),
        P(("dp", "expert"), None),
        P(("dp", "expert"), None),
        P(("dp", "expert"), None),
        P(("dp", "expert"), None),
        P("expert", "dp", None),
        P("expert", "dp", None),
        P("expert", "dp", None),
    )
    return jax.shard_map(
        per_device,
        mesh=mesh,
        in_specs=placed,
        out_specs=(
            P(("dp", "expert"), None),
            P(("dp", "expert"), None),
            P(("dp", "expert"), None),
            P("expert", "dp", None),
        ),
        check_vma=False,
    )
```

```python
import functools
import math

import jax
import jax.numpy as jnp
from jax import lax
from jax.experimental import pallas as pl
from jax.experimental.pallas import tpu as pltpu
from jax.sharding import PartitionSpec as P


BLOCK = 256
STRIDE = 4


def _dot(a, b, over):
    return lax.dot_general(a, b, ((over[:1], over[1:]), ((), ())), preferred_element_type=jnp.float32)


def _fetches(place, shards, which, buffer, sems, steps):
    groups = len(shards)
    return [
        [
            pltpu.make_async_copy(
                shards[k].at[which, :, pl.ds(j * BLOCK, BLOCK)],
                buffer.at[j, (place[0] + k) % groups],
                sems.at[j, k],
            )
            for k in range(groups)
        ]
        for j in range(steps)
    ]


def _start(fetches):
    for copies in fetches:
        for copy in copies:
            copy.start()


def _await(fetches, at):
    for j, copies in enumerate(fetches):

        @pl.when(at == j)
        def _():
            for copy in copies:
                copy.wait()


def _columns(buffer, at):
    return buffer[at].reshape(buffer.shape[1] * buffer.shape[2], BLOCK)


def _hidden_kernel(place, rows, cot, *refs, groups):
    shards, refs = refs[:groups], refs[groups:]
    hidden, slope, activated, send_two, send_one, own_three, own_zero = refs[:7]
    gate_buffer, up_buffer, classes, gate_sems, up_sems = refs[7:]
    at = pl.program_id(0)
    steps = gate_buffer.shape[0]
    gate_copies = _fetches(place, shards, 0, gate_buffer, gate_sems, steps)
    up_copies = _fetches(place, shards, 1, up_buffer, up_sems, steps)

    @pl.when(at == 0)
    def _():
        for j in range(steps):
            _start(gate_copies[j : j + 1])
            _start(up_copies[j : j + 1])

    _await(gate_copies, at)
    pre_gate = _dot(rows[...], _columns(gate_buffer, at), (1, 0))
    _await(up_copies, at)
    pre_up = _dot(rows[...], _columns(up_buffer, at), (1, 0))
    squashed = jax.nn.sigmoid(pre_gate)
    active = pre_gate * squashed
    here = (active * pre_up).astype(jnp.bfloat16)
    hidden[...] = here
    activated[...] = active
    slope[...] = pre_up * squashed * (1.0 + pre_gate * (1.0 - squashed))
    partial = _dot(cot[...], here, (0, 0))
    members, block = classes.shape[1], classes.shape[2]
    for index in range(members * STRIDE):
        classes[index % STRIDE, index // STRIDE] = partial[index * block : (index + 1) * block]
    for shift, target in ((2, send_two), (1, send_one), (3, own_three), (0, own_zero)):
        target[...] = classes[(place[0] + shift) % STRIDE].astype(target.dtype)


def _buffers(names, steps, groups, block):
    return [pltpu.VMEM((steps, groups, block, BLOCK), jnp.bfloat16) for _ in names]


def hidden_and_partial(place, rows, cot, shards):
    slots, features = rows.shape
    groups = len(shards)
    _, block, width = shards[0].shape
    steps = width // BLOCK
    members = groups // STRIDE
    whole = pl.BlockSpec((slots, features), lambda j, place: (0, 0))
    column = pl.BlockSpec((slots, BLOCK), lambda j, place: (0, j))
    part = pl.BlockSpec((members, block, BLOCK), lambda j, place: (0, 0, j))
    part_shape = (members, block, width)
    return pl.pallas_call(
        functools.partial(_hidden_kernel, groups=groups),
        grid_spec=pltpu.PrefetchScalarGridSpec(
            num_scalar_prefetch=1,
            grid=(steps,),
            in_specs=[whole, whole, *[pl.BlockSpec(memory_space=pl.ANY)] * groups],
            out_specs=[column, column, column, part, part, part, part],
            scratch_shapes=[
                *_buffers(("gate", "up"), steps, groups, block),
                pltpu.VMEM((STRIDE, members, block, BLOCK), jnp.float32),
                pltpu.SemaphoreType.DMA((steps, groups)),
                pltpu.SemaphoreType.DMA((steps, groups)),
            ],
        ),
        out_shape=[
            jax.ShapeDtypeStruct((slots, width), jnp.bfloat16),
            jax.ShapeDtypeStruct((slots, width), jnp.float32),
            jax.ShapeDtypeStruct((slots, width), jnp.float32),
            jax.ShapeDtypeStruct(part_shape, jnp.bfloat16),
            jax.ShapeDtypeStruct(part_shape, jnp.bfloat16),
            jax.ShapeDtypeStruct(part_shape, jnp.float32),
            jax.ShapeDtypeStruct(part_shape, jnp.float32),
        ],
        name="hidden_and_partial",
    )(place, rows, cot, *shards)


def _back_kernel(place, hidden, cot, slope, activated, *refs, groups):
    shards, refs = refs[:groups], refs[groups:]
    back, gate_buffer, up_buffer, down_buffer, out_sum, cot_sum, gate_sems, up_sems, down_sems = refs
    at = pl.program_id(0)
    features = cot.shape[1]
    steps = gate_buffer.shape[0]
    gate_copies = _fetches(place, shards, 0, gate_buffer, gate_sems, steps)
    up_copies = _fetches(place, shards, 1, up_buffer, up_sems, steps)
    down_copies = _fetches(place, shards, 2, down_buffer, down_sems, steps)

    @pl.when(at == 0)
    def _():
        for j in range(steps):
            _start(down_copies[j : j + 1])
            _start(gate_copies[j : j + 1])
            _start(up_copies[j : j + 1])

    _await(down_copies, at)
    down = _columns(down_buffer, at)
    hidden_cot = _dot(cot[...], down, (1, 0))
    gate_cot = (hidden_cot * slope[...]).astype(jnp.bfloat16)
    up_cot = (hidden_cot * activated[...]).astype(jnp.bfloat16)
    out_part = _dot(hidden[...], down, (1, 1))
    _await(gate_copies, at)
    _await(up_copies, at)
    cot_part = _dot(gate_cot, _columns(gate_buffer, at), (1, 1)) + _dot(
        up_cot, _columns(up_buffer, at), (1, 1)
    )

    @pl.when(at == 0)
    def _():
        out_sum[...] = out_part
        cot_sum[...] = cot_part

    @pl.when(at > 0)
    def _():
        out_sum[...] += out_part
        cot_sum[...] += cot_part

    @pl.when(at == steps - 1)
    def _():
        back[:, :features] = out_sum[...].astype(jnp.bfloat16)
        back[:, features:] = cot_sum[...].astype(jnp.bfloat16)


def rows_back(place, hidden, cot, slope, activated, shards):
    slots, features = cot.shape
    groups = len(shards)
    _, block, width = shards[0].shape
    steps = width // BLOCK
    column = pl.BlockSpec((slots, BLOCK), lambda j, place: (0, j))
    return pl.pallas_call(
        functools.partial(_back_kernel, groups=groups),
        grid_spec=pltpu.PrefetchScalarGridSpec(
            num_scalar_prefetch=1,
            grid=(steps,),
            in_specs=[
                column,
                pl.BlockSpec((slots, features), lambda j, place: (0, 0)),
                column,
                column,
                *[pl.BlockSpec(memory_space=pl.ANY)] * groups,
            ],
            out_specs=pl.BlockSpec((slots, 2 * features), lambda j, place: (0, 0)),
            scratch_shapes=[
                *_buffers(("gate", "up", "down"), steps, groups, block),
                pltpu.VMEM((slots, features), jnp.float32),
                pltpu.VMEM((slots, features), jnp.float32),
                *[pltpu.SemaphoreType.DMA((steps, groups))] * 3,
            ],
        ),
        out_shape=jax.ShapeDtypeStruct((slots, 2 * features), jnp.bfloat16),
        name="rows_back",
    )(place, hidden, cot, slope, activated, *shards)


def _finish_kernel(slot, gates, second_out, first_grad, second_grad, back, second_in, first_total, gate_grad):
    count, features = second_out.shape
    grad = second_grad[...].astype(jnp.float32)
    combined, cot_sum = 0.0, 0.0
    for k in range(slot.shape[1]):
        numbers = lax.broadcasted_iota(jnp.int32, (count, back.shape[0]), 1)
        chosen = (slot[:, k : k + 1] == numbers).astype(jnp.bfloat16)
        out_row = _dot(chosen, back[:, :features], (1, 0))
        combined += gates[:, k : k + 1] * out_row
        gate_grad[:, k : k + 1] = jnp.sum(grad * out_row, axis=1, keepdims=True)
        cot_sum += _dot(chosen, back[:, features:], (1, 0))
    second_in[...] = (second_out[...].astype(jnp.float32) - combined).astype(jnp.bfloat16)
    first_total[...] = (first_grad[...].astype(jnp.float32) + cot_sum).astype(jnp.bfloat16)


def finish(slot, gates, second_out, first_grad, second_grad, back):
    return pl.pallas_call(
        _finish_kernel,
        out_shape=[
            jax.ShapeDtypeStruct(second_out.shape, jnp.bfloat16),
            jax.ShapeDtypeStruct(first_grad.shape, jnp.bfloat16),
            jax.ShapeDtypeStruct(gates.shape, jnp.float32),
        ],
        name="finish",
    )(slot, gates, second_out, first_grad, second_grad, back)


def to_slots(placing, assigned_rows):
    return lax.dot_general(
        placing, assigned_rows, (((0,), (0,)), ((), ())), preferred_element_type=jnp.float32
    ).astype(jnp.bfloat16)


def around_ring(own, groups):
    def ring(by, steps):
        passed, value = [], own
        for _ in range(steps):
            value = lax.ppermute(value, "dp", [(i, (i + by) % groups) for i in range(groups)])
            passed.append(value)
        return passed

    from_below = ring(1, groups // 2)
    from_above = ring(-1, groups - 1 - groups // 2)
    return [own, *from_above, *from_below[::-1]]


def window_reduce(send_two, send_one, own_three, own_zero, groups):
    members = groups // STRIDE
    place = lax.axis_index("dp")

    def moved(value, by):
        return lax.ppermute(value, "dp", [(i, (i + by) % groups) for i in range(groups)])

    from_second = moved(send_two, -1)
    from_below = moved(send_one, 1)
    passed_on = (from_second.astype(jnp.float32) + own_three).astype(jnp.bfloat16)
    from_above = moved(passed_on, -1)
    window = from_above.astype(jnp.float32) + (from_below.astype(jnp.float32) + own_zero)
    rounded = window.astype(jnp.bfloat16)
    member = place // STRIDE

    def block_of(values, ahead):
        return lax.dynamic_index_in_dim(values, (member + ahead) % members, 0, keepdims=False)

    total = block_of(window, 0)
    for ahead in range(1, members):
        total = total + moved(block_of(rounded, ahead), ahead * STRIDE).astype(jnp.float32)
    return total


def per_device(
    first_out, second_out, first_grad, second_grad, routes, gate_values, w_gate, w_up, w_down
):
    count_here = first_out.shape[0]
    feature_count = first_out.shape[1]
    top_count = routes.shape[1]
    owners = lax.axis_size("expert")
    groups = lax.axis_size("dp")
    capacity = min(count_here, 2 * count_here * top_count // owners)
    assigned = count_here * top_count
    slots_all = owners * capacity
    expert_ids = routes.reshape(assigned)
    onehot = (expert_ids[:, None] == jnp.arange(owners, dtype=jnp.int32)[None, :]).astype(jnp.int32)
    before = jnp.cumsum(onehot, axis=0) - onehot
    rank_in = jnp.sum(before * onehot, axis=1)
    slot_index = expert_ids * capacity + rank_in
    placing = (slot_index[:, None] == jnp.arange(slots_all, dtype=jnp.int32)[None, :]).astype(
        jnp.bfloat16
    )
    repeated = jnp.broadcast_to(
        first_out[:, None, :], (count_here, top_count, feature_count)
    ).reshape(assigned, feature_count)
    grad_repeated = jnp.broadcast_to(
        second_grad[:, None, :], (count_here, top_count, feature_count)
    ).reshape(assigned, feature_count)
    cot_rows = (gate_values.reshape(assigned)[:, None] * grad_repeated.astype(jnp.float32)).astype(
        jnp.bfloat16
    )
    send_input = to_slots(placing, repeated).reshape(owners, capacity, feature_count)
    send_cot = to_slots(placing, cot_rows).reshape(owners, capacity, feature_count)
    arrived_input, arrived_cot = (
        lax.all_to_all(send_input, "expert", split_axis=0, concat_axis=0, tiled=True),
        lax.all_to_all(send_cot, "expert", split_axis=0, concat_axis=0, tiled=True),
    )
    rows_in = arrived_input.reshape(slots_all, feature_count)
    rows_cot = arrived_cot.reshape(slots_all, feature_count)
    own = jnp.concatenate([w_gate, w_up, w_down], axis=0)
    shards = around_ring(own, groups)
    place = lax.axis_index("dp").astype(jnp.int32).reshape(1)
    hidden, slope, activated, *parts = hidden_and_partial(place, rows_in, rows_cot, shards)
    back_rows = rows_back(place, hidden, rows_cot, slope, activated, shards)
    back = lax.all_to_all(
        back_rows.reshape(owners, capacity, 2 * feature_count),
        "expert",
        split_axis=0,
        concat_axis=0,
        tiled=True,
    ).reshape(slots_all, 2 * feature_count)
    grad_scale = 1.0 / math.sqrt(count_here * groups)
    w_down_grad = (window_reduce(*parts, groups) * grad_scale)[None]
    second_in, first_total, gate_grad = finish(
        slot_index.reshape(count_here, top_count),
        gate_values,
        second_out,
        first_grad,
        second_grad,
        back,
    )
    return (second_in, first_total, gate_grad, w_down_grad)


def solution(mesh):
    placed = (
        P(("dp", "expert"), None),
        P(("dp", "expert"), None),
        P(("dp", "expert"), None),
        P(("dp", "expert"), None),
        P(("dp", "expert"), None),
        P(("dp", "expert"), None),
        P("expert", "dp", None),
        P("expert", "dp", None),
        P("expert", "dp", None),
    )
    return jax.shard_map(
        per_device,
        mesh=mesh,
        in_specs=placed,
        out_specs=(
            P(("dp", "expert"), None),
            P(("dp", "expert"), None),
            P(("dp", "expert"), None),
            P("expert", "dp", None),
        ),
        check_vma=False,
    )
```

```python
import math

import jax
import jax.numpy as jnp
from jax import lax
from jax.experimental import pallas as pl
from jax.experimental.pallas import tpu as pltpu
from jax.sharding import PartitionSpec as P


BLOCK = 256
STRIDE = 4


def _dot(a, b, over):
    return lax.dot_general(a, b, ((over[:1], over[1:]), ((), ())), preferred_element_type=jnp.float32)


def _hidden_kernel(
    place, rows, cot, gate, up, hidden, slope, activated, send_two, send_one, own_three, own_zero, classes
):
    pre_gate = _dot(rows[...], gate[...], (1, 0))
    pre_up = _dot(rows[...], up[...], (1, 0))
    squashed = jax.nn.sigmoid(pre_gate)
    active = pre_gate * squashed
    here = (active * pre_up).astype(jnp.bfloat16)
    hidden[...] = here
    activated[...] = active
    slope[...] = pre_up * squashed * (1.0 + pre_gate * (1.0 - squashed))
    partial = _dot(cot[...], here, (1, 0))
    members, block = classes.shape[1], classes.shape[2]
    for index in range(members * STRIDE):
        classes[index % STRIDE, index // STRIDE] = partial[index * block : (index + 1) * block]
    for shift, target in ((2, send_two), (1, send_one), (3, own_three), (0, own_zero)):
        target[...] = classes[(place[0] + shift) % STRIDE].astype(target.dtype)


def hidden_and_partial(place, rows, cot, mats, groups):
    slots, features = rows.shape
    width = mats.shape[1] // 3
    steps = width // BLOCK
    members, block = groups // STRIDE, features // groups
    whole = pl.BlockSpec((slots, features), lambda j, place: (0, 0))
    column = pl.BlockSpec((slots, BLOCK), lambda j, place: (0, j))
    part = pl.BlockSpec((members, block, BLOCK), lambda j, place: (0, 0, j))
    part_shape = (members, block, width)
    return pl.pallas_call(
        _hidden_kernel,
        grid_spec=pltpu.PrefetchScalarGridSpec(
            num_scalar_prefetch=1,
            grid=(steps,),
            in_specs=[
                whole,
                pl.BlockSpec((features, slots), lambda j, place: (0, 0)),
                pl.BlockSpec((features, BLOCK), lambda j, place: (0, j)),
                pl.BlockSpec((features, BLOCK), lambda j, place: (0, j + steps)),
            ],
            out_specs=[column, column, column, part, part, part, part],
            scratch_shapes=[pltpu.VMEM((STRIDE, members, block, BLOCK), jnp.float32)],
        ),
        out_shape=[
            jax.ShapeDtypeStruct((slots, width), jnp.bfloat16),
            jax.ShapeDtypeStruct((slots, width), jnp.float32),
            jax.ShapeDtypeStruct((slots, width), jnp.float32),
            jax.ShapeDtypeStruct(part_shape, jnp.bfloat16),
            jax.ShapeDtypeStruct(part_shape, jnp.bfloat16),
            jax.ShapeDtypeStruct(part_shape, jnp.float32),
            jax.ShapeDtypeStruct(part_shape, jnp.float32),
        ],
        name="hidden_and_partial",
    )(place, rows, cot, mats, mats)


def _back_kernel(hidden, cot, slope, activated, gate, up, down_mat, back, out_sum, cot_sum):
    at = pl.program_id(0)
    features = cot.shape[1]
    down = down_mat[...]
    hidden_cot = _dot(cot[...], down, (1, 0))
    gate_cot = (hidden_cot * slope[...]).astype(jnp.bfloat16)
    up_cot = (hidden_cot * activated[...]).astype(jnp.bfloat16)
    out_part = _dot(hidden[...], down, (1, 1))
    cot_part = _dot(gate_cot, gate[...], (1, 1)) + _dot(up_cot, up[...], (1, 1))

    @pl.when(at == 0)
    def _():
        out_sum[...] = out_part
        cot_sum[...] = cot_part

    @pl.when(at > 0)
    def _():
        out_sum[...] += out_part
        cot_sum[...] += cot_part

    @pl.when(at == pl.num_programs(0) - 1)
    def _():
        back[:, :features] = out_sum[...].astype(jnp.bfloat16)
        back[:, features:] = cot_sum[...].astype(jnp.bfloat16)


def rows_back(hidden, cot, slope, activated, mats):
    slots, features = cot.shape
    steps = hidden.shape[1] // BLOCK
    column = pl.BlockSpec((slots, BLOCK), lambda j: (0, j))
    return pl.pallas_call(
        _back_kernel,
        grid=(steps,),
        in_specs=[
            column,
            pl.BlockSpec((slots, features), lambda j: (0, 0)),
            column,
            column,
            pl.BlockSpec((features, BLOCK), lambda j: (0, j)),
            pl.BlockSpec((features, BLOCK), lambda j: (0, j + steps)),
            pl.BlockSpec((features, BLOCK), lambda j: (0, j + 2 * steps)),
        ],
        out_specs=pl.BlockSpec((slots, 2 * features), lambda j: (0, 0)),
        out_shape=jax.ShapeDtypeStruct((slots, 2 * features), jnp.bfloat16),
        scratch_shapes=[
            pltpu.VMEM((slots, features), jnp.float32),
            pltpu.VMEM((slots, features), jnp.float32),
        ],
        name="rows_back",
    )(hidden, cot, slope, activated, mats, mats, mats)


def _finish_kernel(slot, gates, second_out, first_grad, second_grad, back, second_in, first_total, gate_grad):
    count, features = second_out.shape
    grad = second_grad[...].astype(jnp.float32)
    combined, cot_sum = 0.0, 0.0
    for k in range(slot.shape[1]):
        numbers = lax.broadcasted_iota(jnp.int32, (count, back.shape[0]), 1)
        chosen = (slot[:, k : k + 1] == numbers).astype(jnp.bfloat16)
        out_row = _dot(chosen, back[:, :features], (1, 0))
        combined += gates[:, k : k + 1] * out_row
        gate_grad[:, k : k + 1] = jnp.sum(grad * out_row, axis=1, keepdims=True)
        cot_sum += _dot(chosen, back[:, features:], (1, 0))
    second_in[...] = (second_out[...].astype(jnp.float32) - combined).astype(jnp.bfloat16)
    first_total[...] = (first_grad[...].astype(jnp.float32) + cot_sum).astype(jnp.bfloat16)


def finish(slot, gates, second_out, first_grad, second_grad, back):
    held = pl.BlockSpec(memory_space=pltpu.VMEM)
    return pl.pallas_call(
        _finish_kernel,
        in_specs=[held] * 6,
        out_specs=[held] * 3,
        out_shape=[
            jax.ShapeDtypeStruct(second_out.shape, jnp.bfloat16),
            jax.ShapeDtypeStruct(first_grad.shape, jnp.bfloat16),
            jax.ShapeDtypeStruct(gates.shape, jnp.float32),
        ],
        name="finish",
    )(slot, gates, second_out, first_grad, second_grad, back)


def to_slots(placing, assigned_rows):
    return lax.dot_general(
        placing, assigned_rows, (((0,), (0,)), ((), ())), preferred_element_type=jnp.float32
    ).astype(jnp.bfloat16)


def window_reduce(send_two, send_one, own_three, own_zero, groups):
    members = groups // STRIDE
    place = lax.axis_index("dp")

    def moved(value, by):
        return lax.ppermute(value, "dp", [(i, (i + by) % groups) for i in range(groups)])

    from_second = moved(send_two, -1)
    from_below = moved(send_one, 1)
    passed_on = (from_second.astype(jnp.float32) + own_three).astype(jnp.bfloat16)
    from_above = moved(passed_on, -1)
    window = from_above.astype(jnp.float32) + (from_below.astype(jnp.float32) + own_zero)
    rounded = window.astype(jnp.bfloat16)
    member = place // STRIDE

    def block_of(values, ahead):
        return lax.dynamic_index_in_dim(values, (member + ahead) % members, 0, keepdims=False)

    total = block_of(window, 0)
    for ahead in range(1, members):
        total = total + moved(block_of(rounded, ahead), ahead * STRIDE).astype(jnp.float32)
    return total


def per_device(
    first_out, second_out, first_grad, second_grad, routes, gate_values, w_gate, w_up, w_down
):
    count_here = first_out.shape[0]
    feature_count = first_out.shape[1]
    top_count = routes.shape[1]
    owners = lax.axis_size("expert")
    groups = lax.axis_size("dp")
    capacity = min(count_here, 2 * count_here * top_count // owners)
    assigned = count_here * top_count
    slots_all = owners * capacity
    expert_ids = routes.reshape(assigned)
    onehot = (expert_ids[:, None] == jnp.arange(owners, dtype=jnp.int32)[None, :]).astype(jnp.int32)
    before = jnp.cumsum(onehot, axis=0) - onehot
    rank_in = jnp.sum(before * onehot, axis=1)
    slot_index = expert_ids * capacity + rank_in
    placing = (slot_index[:, None] == jnp.arange(slots_all, dtype=jnp.int32)[None, :]).astype(
        jnp.bfloat16
    )
    repeated = jnp.broadcast_to(
        first_out[:, None, :], (count_here, top_count, feature_count)
    ).reshape(assigned, feature_count)
    grad_repeated = jnp.broadcast_to(
        second_grad[:, None, :], (count_here, top_count, feature_count)
    ).reshape(assigned, feature_count)
    cot_rows = (gate_values.reshape(assigned)[:, None] * grad_repeated.astype(jnp.float32)).astype(
        jnp.bfloat16
    )
    send_input = to_slots(placing, repeated).reshape(owners, capacity, feature_count)
    send_cot = to_slots(placing, cot_rows).reshape(owners, capacity, feature_count)
    arrived_input, arrived_cot = (
        lax.all_to_all(send_input, "expert", split_axis=0, concat_axis=0, tiled=True),
        lax.all_to_all(send_cot, "expert", split_axis=0, concat_axis=0, tiled=True),
    )
    rows_in = arrived_input.reshape(slots_all, feature_count)
    rows_cot = arrived_cot.reshape(slots_all, feature_count)
    shards = jnp.concatenate([w_gate[0], w_up[0], w_down[0]], axis=1)
    mats = lax.all_gather(shards, "dp", axis=0, tiled=True)
    place = lax.axis_index("dp").astype(jnp.int32).reshape(1)
    hidden, slope, activated, *parts = hidden_and_partial(place, rows_in, rows_cot.T, mats, groups)
    back_rows = rows_back(hidden, rows_cot, slope, activated, mats)
    back = lax.all_to_all(
        back_rows.reshape(owners, capacity, 2 * feature_count),
        "expert",
        split_axis=0,
        concat_axis=0,
        tiled=True,
    ).reshape(slots_all, 2 * feature_count)
    grad_scale = 1.0 / math.sqrt(count_here * groups)
    w_down_grad = (window_reduce(*parts, groups) * grad_scale)[None]
    second_in, first_total, gate_grad = finish(
        slot_index.reshape(count_here, top_count),
        gate_values,
        second_out,
        first_grad,
        second_grad,
        back,
    )
    return (second_in, first_total, gate_grad, w_down_grad)


def solution(mesh):
    placed = (
        P(("dp", "expert"), None),
        P(("dp", "expert"), None),
        P(("dp", "expert"), None),
        P(("dp", "expert"), None),
        P(("dp", "expert"), None),
        P(("dp", "expert"), None),
        P("expert", "dp", None),
        P("expert", "dp", None),
        P("expert", "dp", None),
    )
    return jax.shard_map(
        per_device,
        mesh=mesh,
        in_specs=placed,
        out_specs=(
            P(("dp", "expert"), None),
            P(("dp", "expert"), None),
            P(("dp", "expert"), None),
            P("expert", "dp", None),
        ),
        check_vma=False,
    )
```

```python
import math

import jax
import jax.numpy as jnp
from jax import lax
from jax.experimental import pallas as pl
from jax.experimental.pallas import tpu as pltpu
from jax.sharding import PartitionSpec as P


BLOCK = 256
STRIDE = 4


def _dot(a, b, over):
    return lax.dot_general(a, b, ((over[:1], over[1:]), ((), ())), preferred_element_type=jnp.float32)


def _hidden_kernel(
    place, rows, cot, gate, up, hidden, slope, activated, send_two, send_one, own_three, own_zero, classes
):
    pre_gate = _dot(rows[...], gate[...], (1, 0))
    pre_up = _dot(rows[...], up[...], (1, 0))
    squashed = jax.nn.sigmoid(pre_gate)
    active = pre_gate * squashed
    here = (active * pre_up).astype(jnp.bfloat16)
    hidden[...] = here
    activated[...] = active
    slope[...] = pre_up * squashed * (1.0 + pre_gate * (1.0 - squashed))
    partial = _dot(cot[...], here, (1, 0))
    members, block = classes.shape[1], classes.shape[2]
    for index in range(members * STRIDE):
        classes[index % STRIDE, index // STRIDE] = partial[index * block : (index + 1) * block]
    groups = members * STRIDE
    for ahead, target in ((-2, send_two), (1, send_one), (-1, own_three), (0, own_zero)):
        owner = (place[0] + ahead + groups) % groups
        for m in range(members):
            block_at = (owner // STRIDE + m) % members
            target[m] = classes[owner % STRIDE, block_at].astype(target.dtype)


def hidden_and_partial(place, rows, cot, mats, groups):
    slots, features = rows.shape
    width = mats.shape[1] // 3
    steps = width // BLOCK
    members, block = groups // STRIDE, features // groups
    held = pl.BlockSpec(memory_space=pltpu.VMEM)
    column = pl.BlockSpec((slots, BLOCK), lambda j, place: (0, j))
    part = pl.BlockSpec((members, block, BLOCK), lambda j, place: (0, 0, j))
    part_shape = (members, block, width)
    return pl.pallas_call(
        _hidden_kernel,
        grid_spec=pltpu.PrefetchScalarGridSpec(
            num_scalar_prefetch=1,
            grid=(steps,),
            in_specs=[
                held,
                held,
                pl.BlockSpec((features, BLOCK), lambda j, place: (0, j)),
                pl.BlockSpec((features, BLOCK), lambda j, place: (0, j + steps)),
            ],
            out_specs=[column, column, column, part, part, part, part],
            scratch_shapes=[pltpu.VMEM((STRIDE, members, block, BLOCK), jnp.float32)],
        ),
        out_shape=[
            jax.ShapeDtypeStruct((slots, width), jnp.bfloat16),
            jax.ShapeDtypeStruct((slots, width), jnp.float32),
            jax.ShapeDtypeStruct((slots, width), jnp.float32),
            jax.ShapeDtypeStruct(part_shape, jnp.bfloat16),
            jax.ShapeDtypeStruct(part_shape, jnp.bfloat16),
            jax.ShapeDtypeStruct(part_shape, jnp.float32),
            jax.ShapeDtypeStruct(part_shape, jnp.float32),
        ],
        name="hidden_and_partial",
    )(place, rows, cot, mats, mats)


def _back_kernel(hidden, cot, slope, activated, gate, up, down_mat, back, out_sum, cot_sum):
    at = pl.program_id(0)
    features = cot.shape[1]
    down = down_mat[...]
    hidden_cot = _dot(cot[...], down, (1, 0))
    gate_cot = (hidden_cot * slope[...]).astype(jnp.bfloat16)
    up_cot = (hidden_cot * activated[...]).astype(jnp.bfloat16)
    out_part = _dot(hidden[...], down, (1, 1))
    cot_part = _dot(gate_cot, gate[...], (1, 1)) + _dot(up_cot, up[...], (1, 1))

    @pl.when(at == 0)
    def _():
        out_sum[...] = out_part
        cot_sum[...] = cot_part

    @pl.when(at > 0)
    def _():
        out_sum[...] += out_part
        cot_sum[...] += cot_part

    @pl.when(at == pl.num_programs(0) - 1)
    def _():
        back[:, :features] = out_sum[...].astype(jnp.bfloat16)
        back[:, features:] = cot_sum[...].astype(jnp.bfloat16)


def rows_back(hidden, cot, slope, activated, mats):
    slots, features = cot.shape
    steps = hidden.shape[1] // BLOCK
    column = pl.BlockSpec((slots, BLOCK), lambda j: (0, j))
    return pl.pallas_call(
        _back_kernel,
        grid=(steps,),
        in_specs=[
            column,
            pl.BlockSpec(memory_space=pltpu.VMEM),
            column,
            column,
            pl.BlockSpec((features, BLOCK), lambda j: (0, j)),
            pl.BlockSpec((features, BLOCK), lambda j: (0, j + steps)),
            pl.BlockSpec((features, BLOCK), lambda j: (0, j + 2 * steps)),
        ],
        out_specs=pl.BlockSpec((slots, 2 * features), lambda j: (0, 0)),
        out_shape=jax.ShapeDtypeStruct((slots, 2 * features), jnp.bfloat16),
        scratch_shapes=[
            pltpu.VMEM((slots, features), jnp.float32),
            pltpu.VMEM((slots, features), jnp.float32),
        ],
        name="rows_back",
    )(hidden, cot, slope, activated, mats, mats, mats)


def _beside_kernel(gate, up, down, out):
    width = gate.shape[2]
    for at, value in enumerate((gate, up, down)):
        out[:, at * width : (at + 1) * width] = value[0]


def side_by_side(gate, up, down):
    return pl.pallas_call(
        _beside_kernel,
        out_shape=jax.ShapeDtypeStruct((gate.shape[1], 3 * gate.shape[2]), gate.dtype),
        name="side_by_side",
    )(gate, up, down)


def _finish_kernel(slot, gates, second_out, first_grad, second_grad, back, second_in, first_total, gate_grad):
    count, features = second_out.shape
    grad = second_grad[...].astype(jnp.float32)
    combined, cot_sum = 0.0, 0.0
    for k in range(slot.shape[1]):
        numbers = lax.broadcasted_iota(jnp.int32, (count, back.shape[0]), 1)
        chosen = (slot[:, k : k + 1] == numbers).astype(jnp.bfloat16)
        out_row = _dot(chosen, back[:, :features], (1, 0))
        combined += gates[:, k : k + 1] * out_row
        gate_grad[k : k + 1, :] = jnp.sum(grad * out_row, axis=1)[None, :]
        cot_sum += _dot(chosen, back[:, features:], (1, 0))
    second_in[...] = (second_out[...].astype(jnp.float32) - combined).astype(jnp.bfloat16)
    first_total[...] = (first_grad[...].astype(jnp.float32) + cot_sum).astype(jnp.bfloat16)


def finish(slot, gates, second_out, first_grad, second_grad, back):
    held = pl.BlockSpec(memory_space=pltpu.VMEM)
    return pl.pallas_call(
        _finish_kernel,
        in_specs=[held] * 6,
        out_specs=[held] * 3,
        out_shape=[
            jax.ShapeDtypeStruct(second_out.shape, jnp.bfloat16),
            jax.ShapeDtypeStruct(first_grad.shape, jnp.bfloat16),
            jax.ShapeDtypeStruct(gates.shape[::-1], jnp.float32),
        ],
        name="finish",
    )(slot, gates, second_out, first_grad, second_grad, back)


def to_slots(placing, assigned_rows):
    return lax.dot_general(
        placing, assigned_rows, (((0,), (0,)), ((), ())), preferred_element_type=jnp.float32
    ).astype(jnp.bfloat16)


def window_reduce(send_two, send_one, own_three, own_zero, groups):
    members = groups // STRIDE

    def moved(value, by):
        return lax.ppermute(value, "dp", [(i, (i + by) % groups) for i in range(groups)])

    from_second = moved(send_two, -1)
    from_below = moved(send_one, 1)
    passed_on = (from_second.astype(jnp.float32) + own_three).astype(jnp.bfloat16)
    from_above = moved(passed_on, -1)
    own = [
        from_above[m].astype(jnp.float32) + (from_below[m].astype(jnp.float32) + own_zero[m])
        for m in range(members)
    ]
    total = own[0]
    for m in range(1, members):
        crossed = moved(own[m].astype(jnp.bfloat16), m * STRIDE)
        total = total + crossed.astype(jnp.float32)
    return total


def per_device(
    first_out, second_out, first_grad, second_grad, routes, gate_values, w_gate, w_up, w_down
):
    count_here = first_out.shape[0]
    feature_count = first_out.shape[1]
    top_count = routes.shape[1]
    owners = lax.axis_size("expert")
    groups = lax.axis_size("dp")
    capacity = min(count_here, 2 * count_here * top_count // owners)
    assigned = count_here * top_count
    slots_all = owners * capacity
    expert_ids = routes.reshape(assigned)
    onehot = (expert_ids[:, None] == jnp.arange(owners, dtype=jnp.int32)[None, :]).astype(jnp.int32)
    before = jnp.cumsum(onehot, axis=0) - onehot
    rank_in = jnp.sum(before * onehot, axis=1)
    slot_index = expert_ids * capacity + rank_in
    placing = (slot_index[:, None] == jnp.arange(slots_all, dtype=jnp.int32)[None, :]).astype(
        jnp.bfloat16
    )
    repeated = jnp.broadcast_to(
        first_out[:, None, :], (count_here, top_count, feature_count)
    ).reshape(assigned, feature_count)
    grad_repeated = jnp.broadcast_to(
        second_grad[:, None, :], (count_here, top_count, feature_count)
    ).reshape(assigned, feature_count)
    cot_rows = (gate_values.reshape(assigned)[:, None] * grad_repeated.astype(jnp.float32)).astype(
        jnp.bfloat16
    )
    send_input = to_slots(placing, repeated).reshape(owners, capacity, feature_count)
    send_cot = to_slots(placing, cot_rows).reshape(owners, capacity, feature_count)
    arrived_input, arrived_cot = (
        lax.all_to_all(send_input, "expert", split_axis=0, concat_axis=0, tiled=True),
        lax.all_to_all(send_cot, "expert", split_axis=0, concat_axis=0, tiled=True),
    )
    rows_in = arrived_input.reshape(slots_all, feature_count)
    rows_cot = arrived_cot.reshape(slots_all, feature_count)
    shards = side_by_side(w_gate, w_up, w_down)
    mats = lax.all_gather(shards, "dp", axis=0, tiled=True)
    place = lax.axis_index("dp").astype(jnp.int32).reshape(1)
    rows_in, rows_cot, cot_turned = (
        pltpu.with_memory_space_constraint(value, pltpu.VMEM)
        for value in (rows_in, rows_cot, rows_cot.T)
    )
    hidden, slope, activated, *parts = hidden_and_partial(place, rows_in, cot_turned, mats, groups)
    back_rows = rows_back(hidden, rows_cot, slope, activated, mats)
    back = lax.all_to_all(
        back_rows.reshape(owners, capacity, 2 * feature_count),
        "expert",
        split_axis=0,
        concat_axis=0,
        tiled=True,
    ).reshape(slots_all, 2 * feature_count)
    back = pltpu.with_memory_space_constraint(back, pltpu.VMEM)
    grad_scale = 1.0 / math.sqrt(count_here * groups)
    w_down_grad = (window_reduce(*parts, groups) * grad_scale)[None]
    second_in, first_total, gate_grad = finish(
        slot_index.reshape(count_here, top_count),
        gate_values,
        second_out,
        first_grad,
        second_grad,
        back,
    )
    return (second_in, first_total, gate_grad.T, w_down_grad)


def solution(mesh):
    placed = (
        P(("dp", "expert"), None),
        P(("dp", "expert"), None),
        P(("dp", "expert"), None),
        P(("dp", "expert"), None),
        P(("dp", "expert"), None),
        P(("dp", "expert"), None),
        P("expert", "dp", None),
        P("expert", "dp", None),
        P("expert", "dp", None),
    )
    return jax.shard_map(
        per_device,
        mesh=mesh,
        in_specs=placed,
        out_specs=(
            P(("dp", "expert"), None),
            P(("dp", "expert"), None),
            P(("dp", "expert"), None),
            P("expert", "dp", None),
        ),
        check_vma=False,
    )
```

```python
import math

import jax
import jax.numpy as jnp
from jax import lax
from jax.experimental import pallas as pl
from jax.experimental.pallas import tpu as pltpu
from jax.sharding import PartitionSpec as P


STRIDE = 4
ROWS_STEP = 64
HIDDEN_BYTES = 48 * 1024 * 1024
BACK_BYTES = 57 * 1024 * 1024
HELD = pl.BlockSpec(memory_space=pltpu.VMEM)


def _dot(a, b, over):
    return lax.dot_general(a, b, ((over[:1], over[1:]), ((), ())), preferred_element_type=jnp.float32)


def in_vmem(value):
    return pltpu.with_memory_space_constraint(value, pltpu.VMEM)


def _hidden_kernel(
    place,
    mats,
    rows,
    cot,
    hidden,
    slope,
    activated,
    send_two,
    send_one,
    own_three,
    own_zero,
    gate,
    up,
    classes,
    sems,
):
    slots, width = hidden.shape
    copies = [
        pltpu.make_async_copy(mats.at[:, pl.ds(k * width, width)], target, sems.at[k])
        for k, target in enumerate((gate, up))
    ]
    for copy in copies:
        copy.start()
    copies[0].wait()
    activated[...] = _dot(rows[...], gate[...], (1, 0))
    copies[1].wait()
    slope[...] = _dot(rows[...], up[...], (1, 0))

    def some_rows(step, carry):
        at = pl.ds(pl.multiple_of(step * ROWS_STEP, ROWS_STEP), ROWS_STEP)
        pre_gate = activated[at, :]
        pre_up = slope[at, :]
        squashed = jax.nn.sigmoid(pre_gate)
        active = pre_gate * squashed
        hidden[at, :] = (active * pre_up).astype(jnp.bfloat16)
        activated[at, :] = active
        slope[at, :] = pre_up * squashed * (1.0 + pre_gate * (1.0 - squashed))
        return carry

    lax.fori_loop(0, slots // ROWS_STEP, some_rows, 0)
    members, block = classes.shape[1], classes.shape[2]
    groups = members * STRIDE
    partial = _dot(cot[...], hidden[...], (1, 0))
    for index in range(groups):
        classes[index % STRIDE, index // STRIDE] = partial[index * block : (index + 1) * block]
    for ahead, target in ((-2, send_two), (1, send_one), (-1, own_three), (0, own_zero)):
        owner = (place[0] + ahead + groups) % groups
        for m in range(members):
            block_at = (owner // STRIDE + m) % members
            target[m] = classes[owner % STRIDE, block_at].astype(target.dtype)


def hidden_and_partial(place, rows, cot, mats, groups):
    slots, features = rows.shape
    width = mats.shape[1] // 3
    members, block = groups // STRIDE, features // groups
    part_shape = (members, block, width)
    results = pl.pallas_call(
        _hidden_kernel,
        in_specs=[
            pl.BlockSpec(memory_space=pltpu.SMEM),
            pl.BlockSpec(memory_space=pltpu.HBM),
            HELD,
            HELD,
        ],
        out_specs=[HELD] * 7,
        out_shape=[
            jax.ShapeDtypeStruct((slots, width), jnp.bfloat16),
            jax.ShapeDtypeStruct((slots, width), jnp.float32),
            jax.ShapeDtypeStruct((slots, width), jnp.float32),
            jax.ShapeDtypeStruct(part_shape, jnp.bfloat16),
            jax.ShapeDtypeStruct(part_shape, jnp.bfloat16),
            jax.ShapeDtypeStruct(part_shape, jnp.float32),
            jax.ShapeDtypeStruct(part_shape, jnp.float32),
        ],
        scratch_shapes=[
            pltpu.VMEM((features, width), jnp.bfloat16),
            pltpu.VMEM((features, width), jnp.bfloat16),
            pltpu.VMEM((STRIDE, members, block, width), jnp.float32),
            pltpu.SemaphoreType.DMA((2,)),
        ],
        compiler_params=pltpu.CompilerParams(vmem_limit_bytes=HIDDEN_BYTES),
        name="hidden_and_partial",
    )(place, mats, rows, cot)
    return [*[in_vmem(value) for value in results[:3]], *results[3:]]


def _back_kernel(mats, hidden, cot, slope, activated, back, down, gate_up, cots, out_rows, cot_rows, sems):
    features, width = down.shape
    leaving = [
        pltpu.make_async_copy(source, back.at[:, pl.ds(k * features, features)], sems.at[2 + k])
        for k, source in enumerate((out_rows, cot_rows))
    ]
    copies = [
        pltpu.make_async_copy(mats.at[:, pl.ds(at, size)], target, sems.at[k])
        for k, (at, size, target) in enumerate(((2 * width, width, down), (0, 2 * width, gate_up)))
    ]
    for copy in copies:
        copy.start()
    copies[0].wait()
    hidden_cot = _dot(cot[...], down[...], (1, 0))
    cots[:, :width] = (hidden_cot * slope[...]).astype(jnp.bfloat16)
    cots[:, width:] = (hidden_cot * activated[...]).astype(jnp.bfloat16)
    out_rows[...] = _dot(hidden[...], down[...], (1, 1)).astype(jnp.bfloat16)
    leaving[0].start()
    copies[1].wait()
    cot_rows[...] = _dot(cots[...], gate_up[...], (1, 1)).astype(jnp.bfloat16)
    leaving[1].start()
    for copy in leaving:
        copy.wait()


def rows_back(hidden, cot, slope, activated, mats):
    slots, features = cot.shape
    width = hidden.shape[1]
    return pl.pallas_call(
        _back_kernel,
        in_specs=[pl.BlockSpec(memory_space=pltpu.HBM), *[HELD] * 4],
        out_specs=pl.BlockSpec(memory_space=pltpu.HBM),
        out_shape=jax.ShapeDtypeStruct((slots, 2 * features), jnp.bfloat16),
        scratch_shapes=[
            pltpu.VMEM((features, width), jnp.bfloat16),
            pltpu.VMEM((features, 2 * width), jnp.bfloat16),
            pltpu.VMEM((slots, 2 * width), jnp.bfloat16),
            pltpu.VMEM((slots, features), jnp.bfloat16),
            pltpu.VMEM((slots, features), jnp.bfloat16),
            pltpu.SemaphoreType.DMA((4,)),
        ],
        compiler_params=pltpu.CompilerParams(vmem_limit_bytes=BACK_BYTES),
        name="rows_back",
    )(mats, hidden, cot, slope, activated)


def _beside_kernel(gate, up, down, out):
    width = gate.shape[2]
    for at, value in enumerate((gate, up, down)):
        out[:, at * width : (at + 1) * width] = value[0]


def side_by_side(gate, up, down):
    return pl.pallas_call(
        _beside_kernel,
        out_shape=jax.ShapeDtypeStruct((gate.shape[1], 3 * gate.shape[2]), gate.dtype),
        name="side_by_side",
    )(gate, up, down)


def _finish_kernel(slot, gates, second_out, first_grad, second_grad, back, second_in, first_total, gate_grad):
    count, features = second_out.shape
    grad = second_grad[...].astype(jnp.float32)
    combined, cot_sum = 0.0, 0.0
    for k in range(slot.shape[1]):
        numbers = lax.broadcasted_iota(jnp.int32, (count, back.shape[0]), 1)
        chosen = (slot[:, k : k + 1] == numbers).astype(jnp.bfloat16)
        out_row = _dot(chosen, back[:, :features], (1, 0))
        combined += gates[:, k : k + 1] * out_row
        gate_grad[k : k + 1, :] = jnp.sum(grad * out_row, axis=1)[None, :]
        cot_sum += _dot(chosen, back[:, features:], (1, 0))
    second_in[...] = (second_out[...].astype(jnp.float32) - combined).astype(jnp.bfloat16)
    first_total[...] = (first_grad[...].astype(jnp.float32) + cot_sum).astype(jnp.bfloat16)


def finish(slot, gates, second_out, first_grad, second_grad, back):
    return pl.pallas_call(
        _finish_kernel,
        in_specs=[HELD] * 6,
        out_specs=[HELD] * 3,
        out_shape=[
            jax.ShapeDtypeStruct(second_out.shape, jnp.bfloat16),
            jax.ShapeDtypeStruct(first_grad.shape, jnp.bfloat16),
            jax.ShapeDtypeStruct(gates.shape[::-1], jnp.float32),
        ],
        name="finish",
    )(slot, gates, second_out, first_grad, second_grad, back)


def to_slots(placing, assigned_rows):
    return lax.dot_general(
        placing, assigned_rows, (((0,), (0,)), ((), ())), preferred_element_type=jnp.float32
    ).astype(jnp.bfloat16)


def window_reduce(send_two, send_one, own_three, own_zero, groups):
    members = groups // STRIDE

    def moved(value, by):
        return lax.ppermute(value, "dp", [(i, (i + by) % groups) for i in range(groups)])

    from_second = moved(send_two, -1)
    from_below = moved(send_one, 1)
    passed_on = (from_second.astype(jnp.float32) + own_three).astype(jnp.bfloat16)
    from_above = moved(passed_on, -1)
    own = [
        from_above[m].astype(jnp.float32) + (from_below[m].astype(jnp.float32) + own_zero[m])
        for m in range(members)
    ]
    total = own[0]
    for m in range(1, members):
        crossed = moved(own[m].astype(jnp.bfloat16), m * STRIDE)
        total = total + crossed.astype(jnp.float32)
    return total


def per_device(
    first_out, second_out, first_grad, second_grad, routes, gate_values, w_gate, w_up, w_down
):
    count_here = first_out.shape[0]
    feature_count = first_out.shape[1]
    top_count = routes.shape[1]
    owners = lax.axis_size("expert")
    groups = lax.axis_size("dp")
    capacity = min(count_here, 2 * count_here * top_count // owners)
    assigned = count_here * top_count
    slots_all = owners * capacity
    expert_ids = routes.reshape(assigned)
    onehot = (expert_ids[:, None] == jnp.arange(owners, dtype=jnp.int32)[None, :]).astype(jnp.int32)
    before = jnp.cumsum(onehot, axis=0) - onehot
    rank_in = jnp.sum(before * onehot, axis=1)
    slot_index = expert_ids * capacity + rank_in
    placing = (slot_index[:, None] == jnp.arange(slots_all, dtype=jnp.int32)[None, :]).astype(
        jnp.bfloat16
    )
    repeated = jnp.broadcast_to(
        first_out[:, None, :], (count_here, top_count, feature_count)
    ).reshape(assigned, feature_count)
    grad_repeated = jnp.broadcast_to(
        second_grad[:, None, :], (count_here, top_count, feature_count)
    ).reshape(assigned, feature_count)
    cot_rows = (gate_values.reshape(assigned)[:, None] * grad_repeated.astype(jnp.float32)).astype(
        jnp.bfloat16
    )
    send_input = to_slots(placing, repeated).reshape(owners, capacity, feature_count)
    send_cot = to_slots(placing, cot_rows).reshape(owners, capacity, feature_count)
    arrived_input, arrived_cot = (
        lax.all_to_all(send_input, "expert", split_axis=0, concat_axis=0, tiled=True),
        lax.all_to_all(send_cot, "expert", split_axis=0, concat_axis=0, tiled=True),
    )
    rows_in = arrived_input.reshape(slots_all, feature_count)
    rows_cot = arrived_cot.reshape(slots_all, feature_count)
    shards = side_by_side(w_gate, w_up, w_down)
    mats = lax.all_gather(shards, "dp", axis=0, tiled=True)
    mats = pltpu.with_memory_space_constraint(mats, pltpu.HBM)
    place = lax.axis_index("dp").astype(jnp.int32).reshape(1)
    rows_in, rows_cot, cot_turned = (in_vmem(value) for value in (rows_in, rows_cot, rows_cot.T))
    hidden, slope, activated, *parts = hidden_and_partial(place, rows_in, cot_turned, mats, groups)
    back_rows = rows_back(hidden, rows_cot, slope, activated, mats)
    back = lax.all_to_all(
        back_rows.reshape(owners, capacity, 2 * feature_count),
        "expert",
        split_axis=0,
        concat_axis=0,
        tiled=True,
    ).reshape(slots_all, 2 * feature_count)
    back = in_vmem(back)
    grad_scale = 1.0 / math.sqrt(count_here * groups)
    w_down_grad = (window_reduce(*parts, groups) * grad_scale)[None]
    second_in, first_total, gate_grad = finish(
        slot_index.reshape(count_here, top_count),
        gate_values,
        second_out,
        first_grad,
        second_grad,
        back,
    )
    return (second_in, first_total, gate_grad.T, w_down_grad)


def solution(mesh):
    placed = (
        P(("dp", "expert"), None),
        P(("dp", "expert"), None),
        P(("dp", "expert"), None),
        P(("dp", "expert"), None),
        P(("dp", "expert"), None),
        P(("dp", "expert"), None),
        P("expert", "dp", None),
        P("expert", "dp", None),
        P("expert", "dp", None),
    )
    return jax.shard_map(
        per_device,
        mesh=mesh,
        in_specs=placed,
        out_specs=(
            P(("dp", "expert"), None),
            P(("dp", "expert"), None),
            P(("dp", "expert"), None),
            P("expert", "dp", None),
        ),
        check_vma=False,
    )
```

```python
import math

import jax
import jax.numpy as jnp
from jax import lax
from jax.experimental import pallas as pl
from jax.experimental.pallas import tpu as pltpu
from jax.sharding import PartitionSpec as P


BLOCK = 256
STRIDE = 4


def _dot(a, b, over):
    return lax.dot_general(a, b, ((over[:1], over[1:]), ((), ())), preferred_element_type=jnp.float32)


def _hidden_kernel(
    place, rows, cot, gate, up, hidden, slope, activated, send_two, send_one, own_three, own_zero, classes
):
    pre_gate = _dot(rows[...], gate[...], (1, 0))
    pre_up = _dot(rows[...], up[...], (1, 0))
    squashed = jax.nn.sigmoid(pre_gate)
    active = pre_gate * squashed
    here = (active * pre_up).astype(jnp.bfloat16)
    hidden[...] = here
    activated[...] = active
    slope[...] = pre_up * squashed * (1.0 + pre_gate * (1.0 - squashed))
    partial = _dot(cot[...], here, (1, 0))
    members, block = classes.shape[1], classes.shape[2]
    for index in range(members * STRIDE):
        classes[index % STRIDE, index // STRIDE] = partial[index * block : (index + 1) * block]
    groups = members * STRIDE
    for ahead, target in ((-2, send_two), (1, send_one), (-1, own_three), (0, own_zero)):
        owner = (place[0] + ahead + groups) % groups
        for m in range(members):
            block_at = (owner // STRIDE + m) % members
            target[m] = classes[owner % STRIDE, block_at].astype(target.dtype)


def hidden_and_partial(place, rows, cot, mats, groups):
    slots, features = rows.shape
    width = mats.shape[1] // 3
    steps = width // BLOCK
    members, block = groups // STRIDE, features // groups
    held = pl.BlockSpec(memory_space=pltpu.VMEM)
    column = pl.BlockSpec((slots, BLOCK), lambda j, place: (0, j))
    part = pl.BlockSpec((members, block, BLOCK), lambda j, place: (0, 0, j))
    part_shape = (members, block, width)
    return pl.pallas_call(
        _hidden_kernel,
        grid_spec=pltpu.PrefetchScalarGridSpec(
            num_scalar_prefetch=1,
            grid=(steps,),
            in_specs=[
                held,
                held,
                pl.BlockSpec((features, BLOCK), lambda j, place: (0, j)),
                pl.BlockSpec((features, BLOCK), lambda j, place: (0, j + steps)),
            ],
            out_specs=[column, column, column, part, part, part, part],
            scratch_shapes=[pltpu.VMEM((STRIDE, members, block, BLOCK), jnp.float32)],
        ),
        out_shape=[
            jax.ShapeDtypeStruct((slots, width), jnp.bfloat16),
            jax.ShapeDtypeStruct((slots, width), jnp.float32),
            jax.ShapeDtypeStruct((slots, width), jnp.float32),
            jax.ShapeDtypeStruct(part_shape, jnp.bfloat16),
            jax.ShapeDtypeStruct(part_shape, jnp.bfloat16),
            jax.ShapeDtypeStruct(part_shape, jnp.float32),
            jax.ShapeDtypeStruct(part_shape, jnp.float32),
        ],
        name="hidden_and_partial",
    )(place, rows, cot, mats, mats)


def _back_kernel(
    mats,
    hidden_far,
    slope_far,
    activated_far,
    cot,
    back,
    down,
    hidden,
    slope,
    activated,
    gate_up,
    cots,
    out_rows,
    cot_rows,
    sems,
):
    features, width = down.shape
    sources = (
        (mats.at[:, pl.ds(2 * width, width)], down),
        (hidden_far, hidden),
        (slope_far, slope),
        (activated_far, activated),
        (mats.at[:, pl.ds(0, 2 * width)], gate_up),
    )
    coming = [pltpu.make_async_copy(*pair, sems.at[k]) for k, pair in enumerate(sources)]
    leaving = [
        pltpu.make_async_copy(source, back.at[:, pl.ds(k * features, features)], sems.at[5 + k])
        for k, source in enumerate((out_rows, cot_rows))
    ]
    for copy in coming:
        copy.start()
    coming[0].wait()
    hidden_cot = _dot(cot[...], down[...], (1, 0))
    coming[1].wait()
    out_rows[...] = _dot(hidden[...], down[...], (1, 1)).astype(jnp.bfloat16)
    leaving[0].start()
    coming[2].wait()
    coming[3].wait()
    cots[:, :width] = (hidden_cot * slope[...]).astype(jnp.bfloat16)
    cots[:, width:] = (hidden_cot * activated[...]).astype(jnp.bfloat16)
    coming[4].wait()
    cot_rows[...] = _dot(cots[...], gate_up[...], (1, 1)).astype(jnp.bfloat16)
    leaving[1].start()
    for copy in leaving:
        copy.wait()


def rows_back(hidden, cot, slope, activated, mats):
    slots, features = cot.shape
    width = hidden.shape[1]
    far = pl.BlockSpec(memory_space=pltpu.HBM)
    return pl.pallas_call(
        _back_kernel,
        in_specs=[far, far, far, far, pl.BlockSpec(memory_space=pltpu.VMEM)],
        out_specs=far,
        out_shape=jax.ShapeDtypeStruct((slots, 2 * features), jnp.bfloat16),
        scratch_shapes=[
            pltpu.VMEM((features, width), jnp.bfloat16),
            pltpu.VMEM((slots, width), jnp.bfloat16),
            pltpu.VMEM((slots, width), jnp.float32),
            pltpu.VMEM((slots, width), jnp.float32),
            pltpu.VMEM((features, 2 * width), jnp.bfloat16),
            pltpu.VMEM((slots, 2 * width), jnp.bfloat16),
            pltpu.VMEM((slots, features), jnp.bfloat16),
            pltpu.VMEM((slots, features), jnp.bfloat16),
            pltpu.SemaphoreType.DMA((7,)),
        ],
        name="rows_back",
    )(mats, hidden, slope, activated, cot)


def _beside_kernel(gate, up, down, out):
    width = gate.shape[2]
    for at, value in enumerate((gate, up, down)):
        out[:, at * width : (at + 1) * width] = value[0]


def side_by_side(gate, up, down):
    return pl.pallas_call(
        _beside_kernel,
        out_shape=jax.ShapeDtypeStruct((gate.shape[1], 3 * gate.shape[2]), gate.dtype),
        name="side_by_side",
    )(gate, up, down)


def _finish_kernel(slot, gates, second_out, first_grad, second_grad, back, second_in, first_total, gate_grad):
    count, features = second_out.shape
    grad = second_grad[...].astype(jnp.float32)
    combined, cot_sum = 0.0, 0.0
    for k in range(slot.shape[1]):
        numbers = lax.broadcasted_iota(jnp.int32, (count, back.shape[0]), 1)
        chosen = (slot[:, k : k + 1] == numbers).astype(jnp.bfloat16)
        out_row = _dot(chosen, back[:, :features], (1, 0))
        combined += gates[:, k : k + 1] * out_row
        gate_grad[k : k + 1, :] = jnp.sum(grad * out_row, axis=1)[None, :]
        cot_sum += _dot(chosen, back[:, features:], (1, 0))
    second_in[...] = (second_out[...].astype(jnp.float32) - combined).astype(jnp.bfloat16)
    first_total[...] = (first_grad[...].astype(jnp.float32) + cot_sum).astype(jnp.bfloat16)


def finish(slot, gates, second_out, first_grad, second_grad, back):
    held = pl.BlockSpec(memory_space=pltpu.VMEM)
    return pl.pallas_call(
        _finish_kernel,
        in_specs=[held] * 6,
        out_specs=[held] * 3,
        out_shape=[
            jax.ShapeDtypeStruct(second_out.shape, jnp.bfloat16),
            jax.ShapeDtypeStruct(first_grad.shape, jnp.bfloat16),
            jax.ShapeDtypeStruct(gates.shape[::-1], jnp.float32),
        ],
        name="finish",
    )(slot, gates, second_out, first_grad, second_grad, back)


def to_slots(placing, assigned_rows):
    return lax.dot_general(
        placing, assigned_rows, (((0,), (0,)), ((), ())), preferred_element_type=jnp.float32
    ).astype(jnp.bfloat16)


def window_reduce(send_two, send_one, own_three, own_zero, groups):
    members = groups // STRIDE

    def moved(value, by):
        return lax.ppermute(value, "dp", [(i, (i + by) % groups) for i in range(groups)])

    from_second = moved(send_two, -1)
    from_below = moved(send_one, 1)
    passed_on = (from_second.astype(jnp.float32) + own_three).astype(jnp.bfloat16)
    from_above = moved(passed_on, -1)
    own = [
        from_above[m].astype(jnp.float32) + (from_below[m].astype(jnp.float32) + own_zero[m])
        for m in range(members)
    ]
    total = own[0]
    for m in range(1, members):
        crossed = moved(own[m].astype(jnp.bfloat16), m * STRIDE)
        total = total + crossed.astype(jnp.float32)
    return total


def per_device(
    first_out, second_out, first_grad, second_grad, routes, gate_values, w_gate, w_up, w_down
):
    count_here = first_out.shape[0]
    feature_count = first_out.shape[1]
    top_count = routes.shape[1]
    owners = lax.axis_size("expert")
    groups = lax.axis_size("dp")
    capacity = min(count_here, 2 * count_here * top_count // owners)
    assigned = count_here * top_count
    slots_all = owners * capacity
    expert_ids = routes.reshape(assigned)
    onehot = (expert_ids[:, None] == jnp.arange(owners, dtype=jnp.int32)[None, :]).astype(jnp.int32)
    before = jnp.cumsum(onehot, axis=0) - onehot
    rank_in = jnp.sum(before * onehot, axis=1)
    slot_index = expert_ids * capacity + rank_in
    placing = (slot_index[:, None] == jnp.arange(slots_all, dtype=jnp.int32)[None, :]).astype(
        jnp.bfloat16
    )
    repeated = jnp.broadcast_to(
        first_out[:, None, :], (count_here, top_count, feature_count)
    ).reshape(assigned, feature_count)
    grad_repeated = jnp.broadcast_to(
        second_grad[:, None, :], (count_here, top_count, feature_count)
    ).reshape(assigned, feature_count)
    cot_rows = (gate_values.reshape(assigned)[:, None] * grad_repeated.astype(jnp.float32)).astype(
        jnp.bfloat16
    )
    send_input = to_slots(placing, repeated).reshape(owners, capacity, feature_count)
    send_cot = to_slots(placing, cot_rows).reshape(owners, capacity, feature_count)
    arrived_input, arrived_cot = (
        lax.all_to_all(send_input, "expert", split_axis=0, concat_axis=0, tiled=True),
        lax.all_to_all(send_cot, "expert", split_axis=0, concat_axis=0, tiled=True),
    )
    rows_in = arrived_input.reshape(slots_all, feature_count)
    rows_cot = arrived_cot.reshape(slots_all, feature_count)
    shards = side_by_side(w_gate, w_up, w_down)
    mats = lax.all_gather(shards, "dp", axis=0, tiled=True)
    place = lax.axis_index("dp").astype(jnp.int32).reshape(1)
    rows_in, rows_cot, cot_turned = (
        pltpu.with_memory_space_constraint(value, pltpu.VMEM)
        for value in (rows_in, rows_cot, rows_cot.T)
    )
    hidden, slope, activated, *parts = hidden_and_partial(place, rows_in, cot_turned, mats, groups)
    back_rows = rows_back(hidden, rows_cot, slope, activated, mats)
    back = lax.all_to_all(
        back_rows.reshape(owners, capacity, 2 * feature_count),
        "expert",
        split_axis=0,
        concat_axis=0,
        tiled=True,
    ).reshape(slots_all, 2 * feature_count)
    back = pltpu.with_memory_space_constraint(back, pltpu.VMEM)
    grad_scale = 1.0 / math.sqrt(count_here * groups)
    w_down_grad = (window_reduce(*parts, groups) * grad_scale)[None]
    second_in, first_total, gate_grad = finish(
        slot_index.reshape(count_here, top_count),
        gate_values,
        second_out,
        first_grad,
        second_grad,
        back,
    )
    return (second_in, first_total, gate_grad.T, w_down_grad)


def solution(mesh):
    placed = (
        P(("dp", "expert"), None),
        P(("dp", "expert"), None),
        P(("dp", "expert"), None),
        P(("dp", "expert"), None),
        P(("dp", "expert"), None),
        P(("dp", "expert"), None),
        P("expert", "dp", None),
        P("expert", "dp", None),
        P("expert", "dp", None),
    )
    return jax.shard_map(
        per_device,
        mesh=mesh,
        in_specs=placed,
        out_specs=(
            P(("dp", "expert"), None),
            P(("dp", "expert"), None),
            P(("dp", "expert"), None),
            P("expert", "dp", None),
        ),
        check_vma=False,
    )
```

```python
import math

import jax
import jax.numpy as jnp
from jax import lax
from jax.experimental import pallas as pl
from jax.experimental.pallas import tpu as pltpu
from jax.sharding import PartitionSpec as P


BLOCK = 256
STRIDE = 4


def _dot(a, b, over):
    return lax.dot_general(a, b, ((over[:1], over[1:]), ((), ())), preferred_element_type=jnp.float32)


def _hidden_kernel(
    place, rows, cot, gate, up, hidden, slope, activated, send_two, send_one, own_three, own_zero, classes
):
    pre_gate = _dot(rows[...], gate[...], (1, 0))
    pre_up = _dot(rows[...], up[...], (1, 0))
    squashed = jax.nn.sigmoid(pre_gate)
    active = pre_gate * squashed
    here = (active * pre_up).astype(jnp.bfloat16)
    hidden[...] = here
    activated[...] = active
    slope[...] = pre_up * squashed * (1.0 + pre_gate * (1.0 - squashed))
    partial = _dot(cot[...], here, (1, 0))
    members, block = classes.shape[1], classes.shape[2]
    for index in range(members * STRIDE):
        classes[index % STRIDE, index // STRIDE] = partial[index * block : (index + 1) * block]
    groups = members * STRIDE
    for ahead, target in ((-2, send_two), (1, send_one), (-1, own_three), (0, own_zero)):
        owner = (place[0] + ahead + groups) % groups
        for m in range(members):
            block_at = (owner // STRIDE + m) % members
            target[m] = classes[owner % STRIDE, block_at].astype(target.dtype)


def hidden_and_partial(place, rows, cot, mats, groups):
    slots, features = rows.shape
    width = mats.shape[1] // 3
    steps = width // BLOCK
    members, block = groups // STRIDE, features // groups
    held = pl.BlockSpec(memory_space=pltpu.VMEM)
    column = pl.BlockSpec((slots, BLOCK), lambda j, place: (0, j))
    part = pl.BlockSpec((members, block, BLOCK), lambda j, place: (0, 0, j))
    part_shape = (members, block, width)
    return pl.pallas_call(
        _hidden_kernel,
        grid_spec=pltpu.PrefetchScalarGridSpec(
            num_scalar_prefetch=1,
            grid=(steps,),
            in_specs=[
                held,
                held,
                pl.BlockSpec((features, BLOCK), lambda j, place: (0, j)),
                pl.BlockSpec((features, BLOCK), lambda j, place: (0, j + steps)),
            ],
            out_specs=[column, column, column, part, part, part, part],
            scratch_shapes=[pltpu.VMEM((STRIDE, members, block, BLOCK), jnp.float32)],
        ),
        out_shape=[
            jax.ShapeDtypeStruct((slots, width), jnp.bfloat16),
            jax.ShapeDtypeStruct((slots, width), jnp.float32),
            jax.ShapeDtypeStruct((slots, width), jnp.float32),
            jax.ShapeDtypeStruct(part_shape, jnp.bfloat16),
            jax.ShapeDtypeStruct(part_shape, jnp.bfloat16),
            jax.ShapeDtypeStruct(part_shape, jnp.float32),
            jax.ShapeDtypeStruct(part_shape, jnp.float32),
        ],
        name="hidden_and_partial",
    )(place, rows, cot, mats, mats)


def _back_kernel(
    mats,
    hidden_far,
    slope_far,
    activated_far,
    cot,
    back,
    down,
    hidden,
    slope,
    activated,
    gate_up,
    cots,
    out_rows,
    cot_rows,
    sems,
):
    features, width = down.shape
    sources = (
        (mats.at[:, pl.ds(2 * width, width)], down),
        (hidden_far, hidden),
        (slope_far, slope),
        (activated_far, activated),
        (mats.at[:, pl.ds(0, 2 * width)], gate_up),
    )
    coming = [pltpu.make_async_copy(*pair, sems.at[k]) for k, pair in enumerate(sources)]
    leaving = [
        pltpu.make_async_copy(source, back.at[:, pl.ds(k * features, features)], sems.at[5 + k])
        for k, source in enumerate((out_rows, cot_rows))
    ]
    for copy in coming:
        copy.start()
    coming[0].wait()
    hidden_cot = _dot(cot[...], down[...], (1, 0))
    coming[1].wait()
    out_rows[...] = _dot(hidden[...], down[...], (1, 1)).astype(jnp.bfloat16)
    leaving[0].start()
    coming[2].wait()
    coming[3].wait()
    cots[:, :width] = (hidden_cot * slope[...]).astype(jnp.bfloat16)
    cots[:, width:] = (hidden_cot * activated[...]).astype(jnp.bfloat16)
    coming[4].wait()
    cot_rows[...] = _dot(cots[...], gate_up[...], (1, 1)).astype(jnp.bfloat16)
    leaving[1].start()
    for copy in leaving:
        copy.wait()


def rows_back(hidden, cot, slope, activated, mats):
    slots, features = cot.shape
    width = hidden.shape[1]
    far = pl.BlockSpec(memory_space=pltpu.HBM)
    return pl.pallas_call(
        _back_kernel,
        in_specs=[far, far, far, far, pl.BlockSpec(memory_space=pltpu.VMEM)],
        out_specs=far,
        out_shape=jax.ShapeDtypeStruct((slots, 2 * features), jnp.bfloat16),
        scratch_shapes=[
            pltpu.VMEM((features, width), jnp.bfloat16),
            pltpu.VMEM((slots, width), jnp.bfloat16),
            pltpu.VMEM((slots, width), jnp.float32),
            pltpu.VMEM((slots, width), jnp.float32),
            pltpu.VMEM((features, 2 * width), jnp.bfloat16),
            pltpu.VMEM((slots, 2 * width), jnp.bfloat16),
            pltpu.VMEM((slots, features), jnp.bfloat16),
            pltpu.VMEM((slots, features), jnp.bfloat16),
            pltpu.SemaphoreType.DMA((7,)),
        ],
        name="rows_back",
    )(mats, hidden, slope, activated, cot)


def _beside_kernel(gate, up, down, out, sems):
    width = gate.shape[2]
    copies = [
        pltpu.make_async_copy(source.at[0], out.at[:, pl.ds(k * width, width)], sems.at[k])
        for k, source in enumerate((gate, up, down))
    ]
    for copy in copies:
        copy.start()
    for copy in copies:
        copy.wait()


def side_by_side(gate, up, down):
    far = pl.BlockSpec(memory_space=pltpu.HBM)
    return pl.pallas_call(
        _beside_kernel,
        in_specs=[far] * 3,
        out_specs=far,
        out_shape=jax.ShapeDtypeStruct((gate.shape[1], 3 * gate.shape[2]), gate.dtype),
        scratch_shapes=[pltpu.SemaphoreType.DMA((3,))],
        name="side_by_side",
    )(gate, up, down)


def _finish_kernel(slot, gates, second_out, first_grad, second_grad, back, second_in, first_total, gate_grad):
    count, features = second_out.shape
    grad = second_grad[...].astype(jnp.float32)
    combined, cot_sum = 0.0, 0.0
    for k in range(slot.shape[1]):
        numbers = lax.broadcasted_iota(jnp.int32, (count, back.shape[0]), 1)
        chosen = (slot[:, k : k + 1] == numbers).astype(jnp.bfloat16)
        out_row = _dot(chosen, back[:, :features], (1, 0))
        combined += gates[:, k : k + 1] * out_row
        gate_grad[k : k + 1, :] = jnp.sum(grad * out_row, axis=1)[None, :]
        cot_sum += _dot(chosen, back[:, features:], (1, 0))
    second_in[...] = (second_out[...].astype(jnp.float32) - combined).astype(jnp.bfloat16)
    first_total[...] = (first_grad[...].astype(jnp.float32) + cot_sum).astype(jnp.bfloat16)


def finish(slot, gates, second_out, first_grad, second_grad, back):
    held = pl.BlockSpec(memory_space=pltpu.VMEM)
    return pl.pallas_call(
        _finish_kernel,
        in_specs=[held] * 6,
        out_specs=[held] * 3,
        out_shape=[
            jax.ShapeDtypeStruct(second_out.shape, jnp.bfloat16),
            jax.ShapeDtypeStruct(first_grad.shape, jnp.bfloat16),
            jax.ShapeDtypeStruct(gates.shape[::-1], jnp.float32),
        ],
        name="finish",
    )(slot, gates, second_out, first_grad, second_grad, back)


def to_slots(placing, assigned_rows):
    return lax.dot_general(
        placing, assigned_rows, (((0,), (0,)), ((), ())), preferred_element_type=jnp.float32
    ).astype(jnp.bfloat16)


def window_reduce(send_two, send_one, own_three, own_zero, groups):
    members = groups // STRIDE

    def moved(value, by):
        return lax.ppermute(value, "dp", [(i, (i + by) % groups) for i in range(groups)])

    from_second = moved(send_two, -1)
    from_below = moved(send_one, 1)
    passed_on = (from_second.astype(jnp.float32) + own_three).astype(jnp.bfloat16)
    from_above = moved(passed_on, -1)
    own = [
        from_above[m].astype(jnp.float32) + (from_below[m].astype(jnp.float32) + own_zero[m])
        for m in range(members)
    ]
    total = own[0]
    for m in range(1, members):
        crossed = moved(own[m].astype(jnp.bfloat16), m * STRIDE)
        total = total + crossed.astype(jnp.float32)
    return total


def per_device(
    first_out, second_out, first_grad, second_grad, routes, gate_values, w_gate, w_up, w_down
):
    count_here = first_out.shape[0]
    feature_count = first_out.shape[1]
    top_count = routes.shape[1]
    owners = lax.axis_size("expert")
    groups = lax.axis_size("dp")
    capacity = min(count_here, 2 * count_here * top_count // owners)
    assigned = count_here * top_count
    slots_all = owners * capacity
    expert_ids = routes.reshape(assigned)
    onehot = (expert_ids[:, None] == jnp.arange(owners, dtype=jnp.int32)[None, :]).astype(jnp.int32)
    before = jnp.cumsum(onehot, axis=0) - onehot
    rank_in = jnp.sum(before * onehot, axis=1)
    slot_index = expert_ids * capacity + rank_in
    placing = (slot_index[:, None] == jnp.arange(slots_all, dtype=jnp.int32)[None, :]).astype(
        jnp.bfloat16
    )
    repeated = jnp.broadcast_to(
        first_out[:, None, :], (count_here, top_count, feature_count)
    ).reshape(assigned, feature_count)
    grad_repeated = jnp.broadcast_to(
        second_grad[:, None, :], (count_here, top_count, feature_count)
    ).reshape(assigned, feature_count)
    cot_rows = (gate_values.reshape(assigned)[:, None] * grad_repeated.astype(jnp.float32)).astype(
        jnp.bfloat16
    )
    send_input = to_slots(placing, repeated).reshape(owners, capacity, feature_count)
    send_cot = to_slots(placing, cot_rows).reshape(owners, capacity, feature_count)
    arrived_input, arrived_cot = (
        lax.all_to_all(send_input, "expert", split_axis=0, concat_axis=0, tiled=True),
        lax.all_to_all(send_cot, "expert", split_axis=0, concat_axis=0, tiled=True),
    )
    rows_in = arrived_input.reshape(slots_all, feature_count)
    rows_cot = arrived_cot.reshape(slots_all, feature_count)
    shards = side_by_side(w_gate, w_up, w_down)
    mats = lax.all_gather(shards, "dp", axis=0, tiled=True)
    place = lax.axis_index("dp").astype(jnp.int32).reshape(1)
    rows_in, rows_cot, cot_turned = (
        pltpu.with_memory_space_constraint(value, pltpu.VMEM)
        for value in (rows_in, rows_cot, rows_cot.T)
    )
    hidden, slope, activated, *parts = hidden_and_partial(place, rows_in, cot_turned, mats, groups)
    back_rows = rows_back(hidden, rows_cot, slope, activated, mats)
    back = lax.all_to_all(
        back_rows.reshape(owners, capacity, 2 * feature_count),
        "expert",
        split_axis=0,
        concat_axis=0,
        tiled=True,
    ).reshape(slots_all, 2 * feature_count)
    back = pltpu.with_memory_space_constraint(back, pltpu.VMEM)
    grad_scale = 1.0 / math.sqrt(count_here * groups)
    w_down_grad = (window_reduce(*parts, groups) * grad_scale)[None]
    second_in, first_total, gate_grad = finish(
        slot_index.reshape(count_here, top_count),
        gate_values,
        second_out,
        first_grad,
        second_grad,
        back,
    )
    return (second_in, first_total, gate_grad.T, w_down_grad)


def solution(mesh):
    placed = (
        P(("dp", "expert"), None),
        P(("dp", "expert"), None),
        P(("dp", "expert"), None),
        P(("dp", "expert"), None),
        P(("dp", "expert"), None),
        P(("dp", "expert"), None),
        P("expert", "dp", None),
        P("expert", "dp", None),
        P("expert", "dp", None),
    )
    return jax.shard_map(
        per_device,
        mesh=mesh,
        in_specs=placed,
        out_specs=(
            P(("dp", "expert"), None),
            P(("dp", "expert"), None),
            P(("dp", "expert"), None),
            P("expert", "dp", None),
        ),
        check_vma=False,
    )
```
